32 devices in a mesh: ctx: 4 (over z), head: 8 (over y, x, core).
Axes of the slice: x: 2, y: 2, z: 4, core: 2. Of those that a mesh axis runs over, the one named last changes fastest.
Arguments:
- layer_input: bfloat16 [1024, 4096], P(('ctx', 'head')), may hold values from -6 to 6
- w_query: bfloat16 [4096, 4096], P('ctx', 'head'), may hold values from -0.09375 to 0.09375
- w_key: bfloat16 [4096, 4096], P('ctx', 'head'), may hold values from -0.09375 to 0.09375
- w_value: bfloat16 [4096, 4096], P('ctx', 'head'), may hold values from -0.09375 to 0.09375
- w_out: bfloat16 [4096, 4096], P('head'), may hold values from -0.09375 to 0.09375
- log_decay: float32 [32, 1024], P('head', 'ctx'), may hold values from -2 to 0
- level_gain: float32 [32, 10], P('head'), may hold values from 0.5 to 2
- level_mask: int32 [8, 10], P('ctx'), may hold values 0 or 1
Outputs:
- layer_out: bfloat16 [1024, 4096], P(('ctx', 'head'))
The draws below stay inside these ranges and needn't reach their ends.
All inputs are finite; a program needn't handle non-finite values. No bound on the sum of `level_mask` on one device may be relied on, other than what follows from the above.
Results may differ from the reference program's by a relative error of at most 0.023.
Values may be sent and summed in bfloat16 or wider, within the bound.
A program may use at most 64 MiB of HBM per device.

```python
import math
import jax
import jax.numpy as jnp
from jax import lax

D = 4096
HEAD_COUNT = 32
HEAD_DIM = 128
TOK_DEV = 256
BLOCK = 128
LEVELS = 10
TOKEN_COUNT = 1024
BLOCKS = 8
N_CTX = 4
N_HEAD = 8


def draw_log_decay(key, part):
    random_subkeys = jax.random.split(key, 7)
    fast_share = 0.5
    fast_head = jax.random.uniform(random_subkeys[0], (HEAD_COUNT,)) < fast_share
    fast_rate = jnp.exp(jax.random.uniform(random_subkeys[1], (HEAD_COUNT,), minval=math.log(1.0 / 50.0), maxval=math.log(1.0 / 30.0)))
    slow_rate = 0.5 / TOKEN_COUNT * jnp.exp(jax.random.uniform(random_subkeys[2], (HEAD_COUNT,), minval=-0.7, maxval=0.7))
    decay_rate = jnp.where(fast_head, fast_rate, slow_rate)
    span_count = TOKEN_COUNT // TOK_DEV
    span_factor = jnp.exp(jax.random.uniform(random_subkeys[3], (HEAD_COUNT, span_count), minval=-0.7, maxval=0.7))
    roughness = jnp.exp(jax.random.uniform(random_subkeys[4], (HEAD_COUNT, TOKEN_COUNT), minval=-0.7, maxval=0.7))
    decay_factor = -decay_rate[:, None] * jnp.repeat(span_factor, TOK_DEV, axis=1) * roughness
    spike_position = jax.random.randint(random_subkeys[5], (HEAD_COUNT, 3), 0, TOKEN_COUNT)
    spike_falloff = jnp.log(jax.random.uniform(random_subkeys[6], (HEAD_COUNT, 3), minval=0.5, maxval=0.8))
    spike_events = jnp.arange(TOKEN_COUNT, dtype=jnp.int32)[None, None, :] == spike_position[:, :, None]
    decay_factor = decay_factor + jnp.sum(jnp.where(spike_events, spike_falloff[:, :, None], 0.0), axis=1)
    return decay_factor.astype(jnp.float32)


def plant(values, rng, low, largest):
    index_at = [jax.random.randint(jax.random.fold_in(rng, axis), (), 0, length) for axis, length in enumerate(values.shape)]
    longest = values.shape.index(max(values.shape))
    next_to = index_at[:longest] + [(index_at[longest] + 1) % values.shape[longest]] + index_at[longest + 1:]
    return values.at[tuple(index_at)].set(low).at[tuple(next_to)].set(largest)


def steps_of(rng, dims, cuts, least, largest):
    loudness, own = 1.0, jax.random.fold_in(rng, 6)
    for axis_at, parts in cuts:
        heights = jnp.exp(jax.random.uniform(jax.random.fold_in(own, axis_at), (parts,), jnp.float32, least / len(cuts), largest / len(cuts)))
        loudness = loudness * jnp.repeat(heights, dims[axis_at] // parts).reshape([-1 if axis == axis_at else 1 for axis in range(len(dims))])
    return loudness


def centred(stream_key, extent, deviation, reach, pieces=(), held_as=jnp.bfloat16):
    level = steps_of(stream_key, extent, pieces, -0.22, 0.18) if pieces else 1.0
    values = jax.random.normal(stream_key, extent, jnp.float32) * deviation * level
    return jnp.minimum(jnp.maximum(values, -reach), reach).astype(held_as)


def setup_inputs(seed: int = 0) -> dict:
    arg_keys = jax.random.split(jax.random.key(seed), 9)
    layer_input = centred(arg_keys[0], (TOKEN_COUNT, D), 1.0, 6.0, ((0, 32),))
    w_query = centred(arg_keys[1], (D, D), D ** -0.5, 0.09375, ((0, 4), (1, 8)))
    w_key = centred(arg_keys[2], (D, D), D ** -0.5, 0.09375, ((0, 4), (1, 8)))
    w_value = centred(arg_keys[3], (D, D), D ** -0.5, 0.09375, ((0, 4), (1, 8)))
    w_out = centred(arg_keys[4], (D, D), D ** -0.5, 0.09375, ((0, 8),))
    log_decay = draw_log_decay(jax.random.fold_in(arg_keys[8], 71), 0)
    level_gain = jnp.clip(jnp.exp(math.log(2.0) - 1.3862944 * jax.random.uniform(arg_keys[6], (HEAD_COUNT, LEVELS), jnp.float32) ** steps_of(arg_keys[6], (HEAD_COUNT, LEVELS), ((0, 8),), -0.2, 0.2)), 0.5, 2.0)
    level_mask = plant((jax.random.randint(arg_keys[7], (BLOCKS, LEVELS), 0, 4) < 3).astype(jnp.int32), jax.random.fold_in(arg_keys[7], 1), 0, 1)
    return {"layer_input": layer_input, "w_query": w_query, "w_key": w_key, "w_value": w_value, "w_out": w_out, "log_decay": log_decay, "level_gain": level_gain, "level_mask": level_mask}


def levels_of(first, second, count):
    mixed = jnp.bitwise_xor(first, second)
    result = jnp.zeros(mixed.shape, jnp.int32)
    for level_bit in range(count):
        result = result + (mixed >= 2 ** level_bit).astype(jnp.int32)
    return result

def unit_rows(block):
    floated = block.astype(jnp.float32)
    return (floated / jnp.sqrt(lax.optimization_barrier(jnp.sum(floated * floated, axis=-1, keepdims=True)) + 1e-06)).astype(jnp.bfloat16)

def reference(layer_input, w_query, w_key, w_value, w_out, log_decay, level_gain, level_mask):
    float_input = layer_input.astype(jnp.float32)

    def project(weight):
        return jnp.dot(float_input, weight.astype(jnp.float32)).astype(jnp.bfloat16)

    def heads_first(array):
        return jnp.transpose(array.reshape(TOKEN_COUNT, HEAD_COUNT, HEAD_DIM), (1, 0, 2))
    query = heads_first(project(w_query))
    keys = heads_first(project(w_key))
    values = heads_first(project(w_value))
    per_span = TOK_DEV // BLOCK
    bit_count = N_CTX.bit_length() - 1
    span_index = jnp.arange(N_CTX, dtype=jnp.int32)
    blocks = span_index[:, None] * per_span + jnp.arange(per_span, dtype=jnp.int32)[None, :]
    level_range = jnp.arange(LEVELS, dtype=jnp.int32)
    near_levels = levels_of(blocks[:, :, None], blocks[:, None, :], LEVELS)
    near_onehot = (near_levels[..., None] == level_range).astype(jnp.float32)
    bit_range = jnp.arange(bit_count, dtype=jnp.int32)
    powers = jnp.left_shift(jnp.ones_like(bit_range), bit_range)
    partner = jnp.bitwise_xor(span_index[:, None], powers[None, :])
    far_levels = levels_of(blocks[:, :, None], (partner * per_span)[:, None, :], LEVELS)
    far_onehot = (far_levels[..., None] == level_range).astype(jnp.float32)
    mask_blocks = level_mask.reshape(N_CTX, per_span, LEVELS).astype(jnp.float32)
    mixed_spans = jnp.bitwise_xor(span_index[:, None], span_index[None, :])
    member = (mixed_spans[..., None] >= powers) & (mixed_spans[..., None] < 2 * powers)
    member = member & (span_index[None, :] < span_index[:, None])[..., None]
    position = jnp.arange(TOK_DEV, dtype=jnp.int32)
    causal = position[:, None] >= position[None, :]

    def one_head(inputs):
        query_head, key_head, value_head, decay_head, gain_head = inputs
        query_unit = unit_rows(query_head.reshape(N_CTX, TOK_DEV, HEAD_DIM))
        key_unit = unit_rows(key_head.reshape(N_CTX, TOK_DEV, HEAD_DIM))
        value_span = value_head.reshape(N_CTX, TOK_DEV, HEAD_DIM).astype(jnp.float32)
        cum = jnp.cumsum(decay_head.reshape(N_CTX, TOK_DEV), axis=1)
        span_total = cum[:, -1]
        block_weight = mask_blocks * gain_head[None, None, :]
        near_block = jnp.einsum('cbl,cbel->cbe', block_weight, near_onehot)
        near_tokens = jnp.repeat(jnp.repeat(near_block, BLOCK, axis=1), BLOCK, axis=2)
        scores = jnp.einsum('ctd,csd->cts', query_unit.astype(jnp.float32), key_unit.astype(jnp.float32))
        spread = cum[:, :, None] - cum[:, None, :]
        decay_factor = jnp.where(causal, jnp.exp(jnp.where(causal, spread, 0.0)), 0.0)
        near_weight = (scores * decay_factor * near_tokens).astype(jnp.bfloat16)
        near_out = jnp.einsum('cts,csd->ctd', near_weight.astype(jnp.float32), value_span)
        decayed_key = (key_unit.astype(jnp.float32) * jnp.exp(span_total[:, None] - cum)[:, :, None]).astype(jnp.bfloat16)
        span_state = jnp.einsum('ctd,cte->cde', decayed_key.astype(jnp.float32), value_span)
        inclusive = jnp.cumsum(span_total)
        between = (inclusive - span_total)[:, None] - inclusive[None, :]
        coeff = jnp.where(member, jnp.exp(jnp.where(member, between[..., None], 0.0)), 0.0)
        carried = jnp.einsum('cnm,nde->cmde', coeff, span_state, precision=lax.Precision.HIGHEST)
        far_block = jnp.einsum('cbl,cbml->cbm', block_weight, far_onehot)
        far_tokens = jnp.repeat(far_block, BLOCK, axis=1)
        scaled = query_unit.astype(jnp.float32) * jnp.exp(cum)[:, :, None]
        reached = jnp.einsum('ctd,cmde->ctme', scaled, carried, precision=lax.Precision.HIGHEST)
        far_out = jnp.einsum('ctme,ctm->cte', reached, far_tokens, precision=lax.Precision.HIGHEST)
        return (near_out + far_out).astype(jnp.bfloat16).reshape(TOKEN_COUNT, HEAD_DIM)
    heads = lax.map(one_head, (query, keys, values, log_decay, level_gain))
    heads_out = jnp.transpose(heads, (1, 0, 2)).reshape(TOKEN_COUNT, D)
    group_width = D // N_HEAD
    grouped = jnp.transpose(heads_out.reshape(TOKEN_COUNT, N_HEAD, group_width), (1, 0, 2))
    weight_groups = w_out.reshape(N_HEAD, group_width, D)

    def add_group(total, pair):
        product = jnp.dot(pair[0].astype(jnp.float32), pair[1].astype(jnp.float32))
        rounded = lax.optimization_barrier(product.astype(jnp.bfloat16)).astype(jnp.float32)
        return (total + rounded, None)
    summed, unused = lax.scan(add_group, jnp.zeros((TOKEN_COUNT, D), jnp.float32), (grouped, weight_groups))
    return summed.astype(jnp.bfloat16)
```

```python
import functools

import jax
import jax.numpy as jnp
from jax import lax
from jax.experimental import pallas as pl
from jax.experimental.pallas import tpu as pltpu
from jax.sharding import PartitionSpec as P

HEAD_DIM = 128
BLOCK = 128
LAG = 2
CHUNKS = 4
MESH = pl.DeviceIdType.MESH


def flipped(index, mask):
    bit = 1
    while bit <= mask:
        if mask & bit:
            index = index + bit - 2 * bit * ((index // bit) % 2)
        bit *= 2
    return index


def subsets(bits):
    masks = [0]
    for bit in bits:
        masks = masks + [mask | bit for mask in masks]
    return masks


def bits_of(count):
    return [2**k for k in range(count.bit_length() - 1)]


def unit(block):
    floated = block.astype(jnp.float32)
    return (floated * lax.rsqrt(jnp.sum(floated * floated, axis=-1, keepdims=True) + 1e-06)).astype(jnp.bfloat16)


def lanes(head):
    return slice(head * HEAD_DIM, (head + 1) * HEAD_DIM)


def pair(a, e):
    return a * (a + 1) // 2 + e


def layer_kernel(
    spans, heads, x_ref, wq_ref, wk_ref, wv_ref, w_out_ref, decay_ref, gain_ref, mask_ref, out_ref,
    xs, weight, part, inbox, aux_own, aux_all, cum, cum_t, shape, fade, reach, keys, state, effect,
    ho_out, ho, w_out, share, arrived,
    w_sem, wo_sem, z_send, z_recv, own_sem, g_send, g_recv, p_send, p_recv, a_send, a_recv, h_send, h_recv, s_send, s_recv,
):
    me, lane = lax.axis_index("ctx"), lax.axis_index("head")
    rows = x_ref.shape[0]
    sides, _, depth, width = weight.shape
    own_heads = width // HEAD_DIM
    tokens = heads * rows
    per_span = tokens // BLOCK
    blocks_of_rows = BLOCK // rows
    tiles, kv_tiles = 3 * per_span * spans, 2 * per_span * spans
    chunks, chunk = CHUNKS, w_out.shape[-1]
    bits, span_bits = bits_of(heads), bits_of(spans)
    last = spans - 1
    edge = (me == 0) | (me == last)
    my_side = jnp.where(me == 0, 0, sides - 1)
    owner = edge if sides == 2 else me == 0

    def columns(span):
        return x_ref.at[:, pl.ds(pl.multiple_of(span * depth, depth), depth)]

    own = pltpu.make_async_copy(columns(me), xs.at[me, lane], own_sem)
    own.start()
    loads = [
        pltpu.make_async_copy(ref.at[:, pl.ds(side * width, width)], weight.at[side, k], w_sem.at[side, k])
        for k, ref in ((1, wk_ref), (2, wv_ref), (0, wq_ref))
        for side in range(sides)
    ]
    out_loads = [
        pltpu.make_async_copy(w_out_ref.at[:, pl.ds(j * chunk, chunk)], w_out.at[j], wo_sem.at[j]) for j in range(chunks)
    ]
    for load in loads:
        load.start()

    barrier = pltpu.get_barrier_semaphore()
    for ahead in range(1, spans):
        pl.semaphore_signal(barrier, inc=1, device_id={"ctx": lax.rem(me + ahead, spans)}, device_id_type=MESH)
    for bit in bits:
        pl.semaphore_signal(barrier, inc=1, device_id={"head": flipped(lane, bit)}, device_id_type=MESH)
    aux_own[...] = jnp.zeros_like(aux_own)
    for side in range(sides):
        aux_own[side, :own_heads, :] = decay_ref[side * own_heads : (side + 1) * own_heads, :]
        aux_own[side, own_heads : own_heads + per_span, : mask_ref.shape[1]] = mask_ref[...].astype(jnp.float32)
    pl.semaphore_wait(barrier, spans - 1 + len(bits))

    def exchange(span, source):
        return pltpu.make_async_remote_copy(
            src_ref=columns(span), dst_ref=xs.at[source, lane],
            send_sem=z_send.at[span], recv_sem=z_recv.at[source],
            device_id={"ctx": span}, device_id_type=MESH,
        )

    def send_rows():
        for distance in range(1, spans):

            @pl.when(me + distance < spans)
            def _():
                exchange(me + distance, me).start()

            @pl.when(me - distance >= 0)
            def _():
                exchange(me - distance, me).start()

    def send_aux(side):
        return pltpu.make_async_remote_copy(
            src_ref=aux_own.at[side], dst_ref=aux_all.at[me],
            send_sem=a_send.at[side], recv_sem=a_recv.at[me],
            device_id={"ctx": side * last}, device_id_type=MESH,
        )

    def take_aux(span):
        pltpu.make_async_remote_copy(
            src_ref=aux_own.at[0], dst_ref=aux_all.at[span],
            send_sem=a_send.at[0], recv_sem=a_recv.at[span],
            device_id={"ctx": lax.rem(me + 1, spans)}, device_id_type=MESH,
        ).wait_recv()

    pl.when(edge)(send_rows)

    def gather(span, mask, bit):
        block = xs.at[span, flipped(lane, mask)]
        return pltpu.make_async_remote_copy(
            src_ref=block, dst_ref=block,
            send_sem=g_send.at[span, mask | bit], recv_sem=g_recv.at[span, mask | bit],
            device_id={"head": flipped(lane, bit)}, device_id_type=MESH,
        )

    def settled(span, mask):
        block = xs.at[span, flipped(lane, mask)]
        return pltpu.make_async_remote_copy(
            src_ref=block, dst_ref=block,
            send_sem=g_send.at[span, mask], recv_sem=g_recv.at[span, mask],
            device_id={"head": flipped(lane, bits[0])}, device_id_type=MESH,
        )

    groups = [sorted({g, last - g}) for g in range((spans + 1) // 2)]
    gather_orders = [bits[1:] + bits[:1], bits[:0:-1] + bits[:1]]

    def advance_gather(group, phase):
        for which, span in enumerate(groups[group]):
            path = gather_orders[which]
            if phase == 0:

                @pl.when(me == span)
                def _():
                    own.wait()

                @pl.when(me != span)
                def _():
                    exchange(span, span).wait_recv()
            else:
                for mask in subsets(path[: phase - 1]):
                    settled(span, mask | path[phase - 1]).wait_recv()
            if phase < len(bits):
                for mask in subsets(path[:phase]):
                    gather(span, mask, path[phase]).start()

    def wave(number):
        for phase in range(len(bits), -1, -1):
            if 0 <= number - phase < len(groups):
                advance_gather(number - phase, phase)

    def column(span, head):
        return span * aux_all.shape[1] + head

    def prepare():
        aux_all[me] = aux_own[my_side]
        for span in range(spans):

            @pl.when(me != span)
            def _():
                take_aux(span)

        logs = aux_all[...].reshape(spans * aux_all.shape[1], tokens)
        first = lax.broadcasted_iota(jnp.int32, (tokens, tokens), 0)
        second = lax.broadcasted_iota(jnp.int32, (tokens, tokens), 1)
        exact = lax.Precision.HIGHEST
        cum[...] = jnp.dot(
            logs, (first <= second).astype(jnp.float32), precision=exact, preferred_element_type=jnp.float32
        )
        cum_t[...] = lax.dot_general(
            (second <= first).astype(jnp.float32), logs, (((1,), (1,)), ((), ())),
            precision=exact, preferred_element_type=jnp.float32,
        )
        for span in range(spans):
            for head in range(own_heads):
                j = column(span, head)
                down, across = cum_t[:, j : j + 1], cum[j : j + 1, :]
                fade[span, head] = jnp.broadcast_to(jnp.exp(across[:, tokens - 1 :] - down), (tokens, HEAD_DIM))
                reach[span, head] = jnp.broadcast_to(jnp.exp(down), (tokens, HEAD_DIM))
                for a in range(per_span):
                    for e in range(a + 1):
                        level = (a ^ e).bit_length()
                        spread = down[a * BLOCK : (a + 1) * BLOCK, :] - across[:, e * BLOCK : (e + 1) * BLOCK]
                        if e == a:
                            causal = lax.broadcasted_iota(jnp.int32, (BLOCK, BLOCK), 0) >= lax.broadcasted_iota(
                                jnp.int32, (BLOCK, BLOCK), 1
                            )
                            decay = jnp.where(causal, jnp.exp(jnp.where(causal, spread, 0.0)), 0.0)
                        else:
                            decay = jnp.exp(spread)
                        shape[span, head, pair(a, e)] = decay * level_weight(span, a, head, level)

    def level_weight(span, a, head, level):
        held = aux_all[span, own_heads + a : own_heads + a + 1, level : level + 1]
        gain = gain_ref[head : head + 1, level : level + 1]
        if sides == 2:
            other = gain_ref[own_heads + head : own_heads + head + 1, level : level + 1]
            gain = jnp.where(my_side == 0, gain, other)
        return held * gain

    def absorb(place):
        span = jnp.where(my_side == 0, last - place, place)
        at = place * 2 * per_span
        for head in range(own_heads):
            total = None
            for b in range(per_span):
                key = unit(part[my_side, at + b, :, lanes(head)])
                keys[span, head, b] = key
                decayed = (key.astype(jnp.float32) * fade[span, head, b * BLOCK : (b + 1) * BLOCK, :]).astype(jnp.bfloat16)
                term = lax.dot_general(
                    decayed, part[my_side, at + per_span + b, :, lanes(head)], (((0,), (0,)), ((), ())),
                    preferred_element_type=jnp.float32,
                )
                total = term if total is None else total + term
            state[span, head] = total

    def combine():
        for head in range(own_heads):
            totals = [cum[column(s, head) : column(s, head) + 1, tokens - 1 :] for s in range(spans)]
            for span in range(spans):
                carried = {}
                between = jnp.zeros_like(totals[0])
                for e in range(span - 1, -1, -1):
                    m = (span ^ e).bit_length() - 1
                    term = state[e, head] * jnp.exp(between)
                    carried[m] = carried[m] + term if m in carried else term
                    between = between + totals[e]
                for a in range(per_span):
                    mixed = jnp.zeros((HEAD_DIM, HEAD_DIM), jnp.float32)
                    for m, held in carried.items():
                        mixed = mixed + held * level_weight(span, a, head, (2**m * per_span).bit_length())
                    effect[span, a, head] = mixed.astype(jnp.bfloat16)

    def hand_over(span, a):
        return pltpu.make_async_remote_copy(
            src_ref=ho_out.at[span, a], dst_ref=ho.at[my_side, a],
            send_sem=h_send.at[span, a], recv_sem=h_recv.at[my_side, a],
            device_id={"ctx": span}, device_id_type=MESH,
        )

    def take_heads(side, a):
        pltpu.make_async_remote_copy(
            src_ref=ho_out.at[0, a], dst_ref=ho.at[side, a],
            send_sem=h_send.at[0, a], recv_sem=h_recv.at[side, a],
            device_id={"ctx": lax.rem(me + 1, spans)}, device_id_type=MESH,
        ).wait_recv()

    def respond(place, a):
        span = jnp.where(my_side == 0, last - place, place)
        at = place * 2 * per_span + per_span
        for head in range(own_heads):
            query = unit(part[my_side, kv_tiles + place * per_span + a, :, lanes(head)])
            far = (query.astype(jnp.float32) * reach[span, head, a * BLOCK : (a + 1) * BLOCK, :]).astype(jnp.bfloat16)
            result = jnp.dot(far, effect[span, a, head], preferred_element_type=jnp.float32)
            for e in range(a + 1):
                scores = lax.dot_general(
                    query, keys[span, head, e], (((1,), (1,)), ((), ())), preferred_element_type=jnp.float32
                )
                shaped = (scores * shape[span, head, pair(a, e)]).astype(jnp.bfloat16)
                result = result + jnp.dot(
                    shaped, part[my_side, at + e, :, lanes(head)], preferred_element_type=jnp.float32
                )
            ho_out[span, a, :, lanes(head)] = result.astype(jnp.bfloat16)

        @pl.when(span == me)
        def _():
            ho[my_side, a] = ho_out[span, a]

        @pl.when(span != me)
        def _():
            hand_over(span, a).start()

    def attend(i):
        place = i // (2 * per_span)

        @pl.when((i < kv_tiles) & (i % (2 * per_span) == 2 * per_span - 1))
        def _():
            absorb(place)

        pl.when(i == kv_tiles - 1)(combine)
        for a in range(per_span):

            @pl.when((i >= kv_tiles) & (i % per_span == a))
            def _():
                respond((i - kv_tiles) // per_span, a)

    def link(side, i):
        step = jnp.where(side == 0, -1, 1)
        return pltpu.make_async_remote_copy(
            src_ref=part.at[side, i], dst_ref=inbox.at[side, i],
            send_sem=p_send.at[side, i], recv_sem=p_recv.at[side, i],
            device_id={"ctx": lax.rem(me + step + spans, spans)}, device_id_type=MESH,
        )

    def place_in_chain(side):
        return jnp.where(side == 0, last - me, me)

    def add_tile(side, t, may_own):
        p = place_in_chain(side)
        i = t - LAG * p

        @pl.when((i >= 0) & (i < tiles))
        def _():
            late = i >= kv_tiles
            pos = jnp.where(late, (i - kv_tiles) // per_span, i // (2 * per_span))
            kind = jnp.where(late, 0, 1 + (i % (2 * per_span)) // per_span)
            span = jnp.where(side == 0, last - pos, pos)
            block = xs[span, pl.ds((i % per_span) * blocks_of_rows, blocks_of_rows)]
            if rows % 16:
                block = block.astype(jnp.float32)
            block = block.reshape(BLOCK, depth).astype(jnp.bfloat16)
            product = jnp.dot(block, weight[side, kind], preferred_element_type=jnp.float32)

            @pl.when(p == 0)
            def _():
                part[side, i] = product.astype(jnp.bfloat16)

            @pl.when(p > 0)
            def _():
                link(side, i).wait_recv()
                part[side, i] = (product + inbox[side, i].astype(jnp.float32)).astype(jnp.bfloat16)

            @pl.when(p < last)
            def _():
                link(side, i).start()

            if may_own:

                @pl.when(p == last)
                def _():
                    attend(i)

    if sides == 2:
        first_side = jnp.where(me < last - me, 1, 0)
        order = [first_side, 1 - first_side]
    else:
        order = [0]

    def steps(start, stop):
        def body(t, carry):
            for which, side in enumerate(order):
                add_tile(side, t, which == sides - 1)
            return carry

        lax.fori_loop(start, stop, body, 0)

    wave(0)

    @pl.when(jnp.logical_not(edge))
    def _():
        send_rows()

    for side in range(sides):

        @pl.when(me != side * last)
        def _():
            send_aux(side).start()

    for number in range(1, len(bits) + 1):
        wave(number)
    for load in loads:
        load.wait()
    for load in out_loads:
        load.start()
    done = 0
    for group in range(1, len(groups)):
        steps(done, done + 2 * per_span)
        done += 2 * per_span
        wave(len(bits) + group)
        if group == 1:
            pl.when(owner)(prepare)
    if len(groups) == 1:
        pl.when(owner)(prepare)
    steps(done, tiles + LAG * last)

    for a in range(per_span):
        for side in range(sides):

            @pl.when(me != side * last)
            def _():
                take_heads(side, a)

    orders = [bits[:1] + bits[1:], bits[:1] + bits[:0:-1]]

    def transfer(j, phase, mask):
        bit = orders[j % 2][phase]
        return pltpu.make_async_remote_copy(
            src_ref=share.at[j, flipped(lane, mask | bit)], dst_ref=arrived.at[j, phase, mask],
            send_sem=s_send.at[j, phase, mask], recv_sem=s_recv.at[j, phase, mask],
            device_id={"head": flipped(lane, bit)}, device_id_type=MESH,
        )

    def advance(j, phase):
        path = orders[j % 2]
        if phase == 0:
            out_loads[j].wait()
            product = None
            for side in range(sides):
                term = jnp.dot(
                    ho[side].reshape(tokens, width), w_out[j, side * width : (side + 1) * width, :],
                    preferred_element_type=jnp.float32,
                )
                product = term if product is None else product + term
            share[j] = product.reshape(heads, rows, chunk).astype(jnp.bfloat16)
        else:
            for mask in subsets(path[phase:]):
                transfer(j, phase - 1, mask).wait_recv()
                place = flipped(lane, mask)
                added = share[j, place].astype(jnp.float32) + arrived[j, phase - 1, mask].astype(jnp.float32)
                if phase < len(bits):
                    share[j, place] = added.astype(jnp.bfloat16)
                else:
                    out_ref[:, pl.ds(j * chunk, chunk)] = added.astype(jnp.bfloat16)
        if phase < len(bits):
            for mask in subsets(path[phase + 1 :]):
                transfer(j, phase, mask).start()

    for j in range(chunks):
        advance(j, 0)
    for number in range(chunks + len(bits) - 1):
        for phase in range(len(bits), 0, -1):
            if 0 <= number + 1 - phase < chunks:
                advance(number + 1 - phase, phase)

    for j in range(chunks):
        for phase in range(len(bits)):
            for mask in subsets(orders[j % 2][phase + 1 :]):
                transfer(j, phase, mask).wait_send()
    for distance in range(1, spans):
        exchange(lax.rem(me + distance, spans), me).wait_send()
    for span in range(spans):
        for mask in range(1, heads):
            settled(span, mask).wait_send()
    for side in range(sides):

        @pl.when(me != side * last)
        def _():
            send_aux(side).wait_send()

        @pl.when(place_in_chain(side) < last)
        def _():
            def drain(i, carry):
                link(side, i).wait_send()
                return carry

            lax.fori_loop(0, tiles, drain, 0)

    for span in range(spans):
        for a in range(per_span):

            @pl.when(owner & (me != span))
            def _():
                hand_over(span, a).wait_send()


def on_device(layer_input, w_query, w_key, w_value, w_out, log_decay, level_gain, level_mask):
    spans, heads = lax.axis_size("ctx"), lax.axis_size("head")
    rows, model = layer_input.shape
    depth, columns = w_query.shape
    local_heads, tokens = log_decay.shape
    sides = 2 if local_heads % 2 == 0 and spans > 1 else 1
    width = columns // sides
    own_heads = local_heads // sides
    per_span = tokens // BLOCK
    tiles = 3 * per_span * spans
    aux_rows = -(-(own_heads + per_span) // 8) * 8
    pairs = per_span * (per_span + 1) // 2
    chunk = model // CHUNKS
    phases = heads.bit_length() - 1
    dma = pltpu.SemaphoreType.DMA
    hbm = pl.BlockSpec(memory_space=pl.ANY)
    vmem = pl.BlockSpec(memory_space=pltpu.VMEM)
    half, full = jnp.bfloat16, jnp.float32
    return pl.pallas_call(
        functools.partial(layer_kernel, spans, heads),
        out_shape=jax.ShapeDtypeStruct((rows, model), half),
        in_specs=[hbm] * 5 + [vmem] * 3,
        out_specs=vmem,
        scratch_shapes=[
            pltpu.VMEM((spans, heads, rows, depth), half),
            pltpu.VMEM((sides, 3, depth, width), half),
            pltpu.VMEM((sides, tiles, BLOCK, width), half),
            pltpu.VMEM((sides, tiles, BLOCK, width), half),
            pltpu.VMEM((sides, aux_rows, tokens), full),
            pltpu.VMEM((spans, aux_rows, tokens), full),
            pltpu.VMEM((spans * aux_rows, tokens), full),
            pltpu.VMEM((tokens, spans * aux_rows), full),
            pltpu.VMEM((spans, own_heads, pairs, BLOCK, BLOCK), full),
            pltpu.VMEM((spans, own_heads, tokens, HEAD_DIM), full),
            pltpu.VMEM((spans, own_heads, tokens, HEAD_DIM), full),
            pltpu.VMEM((spans, own_heads, per_span, BLOCK, HEAD_DIM), half),
            pltpu.VMEM((spans, own_heads, HEAD_DIM, HEAD_DIM), full),
            pltpu.VMEM((spans, per_span, own_heads, HEAD_DIM, HEAD_DIM), half),
            pltpu.VMEM((spans, per_span, BLOCK, width), half),
            pltpu.VMEM((sides, per_span, BLOCK, width), half),
            pltpu.VMEM((CHUNKS, columns, chunk), half),
            pltpu.VMEM((CHUNKS, heads, rows, chunk), half),
            pltpu.VMEM((CHUNKS, phases, heads, rows, chunk), half),
            dma((sides, 3)), dma((CHUNKS,)), dma((spans,)), dma((spans,)), dma,
            dma((spans, heads)), dma((spans, heads)),
            dma((sides, tiles)), dma((sides, tiles)),
            dma((sides,)), dma((spans,)),
            dma((spans, per_span)), dma((sides, per_span)),
            dma((CHUNKS, phases, heads)), dma((CHUNKS, phases, heads)),
        ],
        compiler_params=pltpu.CompilerParams(collective_id=0, has_side_effects=True, vmem_limit_bytes=50 * 2**20),
        name="layer",
    )(layer_input, w_query, w_key, w_value, w_out, log_decay, level_gain, level_mask)


def solution(mesh):
    in_specs = (
        P(("ctx", "head"), None),
        P("ctx", "head"),
        P("ctx", "head"),
        P("ctx", "head"),
        P("head", None),
        P("head", "ctx"),
        P("head", None),
        P("ctx", None),
    )
    out_specs = P(("ctx", "head"), None)
    return jax.shard_map(
        on_device, mesh=mesh, in_specs=in_specs, out_specs=out_specs, check_vma=False
    )
```

```python
import functools

import jax
import jax.numpy as jnp
from jax import lax
from jax.experimental import pallas as pl
from jax.experimental.pallas import tpu as pltpu
from jax.sharding import PartitionSpec as P

HEAD_DIM = 128
BLOCK = 128
LAG = 2
CHUNKS = 4
VMEM_LIMIT = 60 * 2**20
MESH = pl.DeviceIdType.MESH


def flipped(index, mask):
    bit = 1
    while bit <= mask:
        if mask & bit:
            index = index + bit - 2 * bit * ((index // bit) % 2)
        bit *= 2
    return index


def subsets(bits):
    masks = [0]
    for bit in bits:
        masks = masks + [mask | bit for mask in masks]
    return masks


def bits_of(count):
    return [2**k for k in range(count.bit_length() - 1)]


def unit(block):
    floated = block.astype(jnp.float32)
    return (floated * lax.rsqrt(jnp.sum(floated * floated, axis=-1, keepdims=True) + 1e-06)).astype(jnp.bfloat16)


def lanes(head):
    return slice(head * HEAD_DIM, (head + 1) * HEAD_DIM)


def pair(a, e):
    return a * (a + 1) // 2 + e


def layer_kernel(
    spans, heads, x_ref, wq_ref, wk_ref, wv_ref, w_out_ref, decay_in, gain_in, mask_in, out_ref,
    decay_ref, gain_ref, mask_ref,
    xs, weight, part, inbox, aux_own, aux_all, cum, cum_t, shape, fade, reach, keys, state, effect,
    ho_out, ho, w_out, share, arrived,
    small_sem, w_sem, wo_sem, z_send, z_recv, own_sem, g_send, g_recv, p_send, p_recv, a_send, a_recv, h_send, h_recv, s_send, s_recv,
):
    me, lane = lax.axis_index("ctx"), lax.axis_index("head")
    rows = x_ref.shape[0]
    sides, _, depth, width = weight.shape
    own_heads = width // HEAD_DIM
    tokens = heads * rows
    per_span = tokens // BLOCK
    blocks_of_rows = BLOCK // rows
    tiles, kv_tiles = 3 * per_span * spans, 2 * per_span * spans
    chunks, chunk = CHUNKS, w_out.shape[-1]
    bits = bits_of(heads)
    across_chips = subsets(bits[1:])
    partners = across_chips[1:] + bits[:1]
    last = spans - 1
    edge = (me == 0) | (me == last)
    my_side = jnp.where(me == 0, 0, sides - 1)
    owner = edge if sides == 2 else me == 0

    def columns(span):
        return x_ref.at[:, pl.ds(pl.multiple_of(span * depth, depth), depth)]

    own = pltpu.make_async_copy(columns(me), xs.at[me, lane], own_sem)
    own.start()
    loads = [
        pltpu.make_async_copy(ref.at[:, pl.ds(side * width, width)], weight.at[side, k], w_sem.at[side, k])
        for k, ref in ((1, wk_ref), (2, wv_ref), (0, wq_ref))
        for side in range(sides)
    ]
    out_loads = [
        pltpu.make_async_copy(w_out_ref.at[:, pl.ds(j * chunk, chunk)], w_out.at[j], wo_sem.at[j]) for j in range(chunks)
    ]
    small_loads = [
        pltpu.make_async_copy(source, target, small_sem.at[k])
        for k, (source, target) in enumerate(((decay_in, decay_ref), (gain_in, gain_ref), (mask_in, mask_ref)))
    ]
    for load in loads + small_loads:
        load.start()

    barrier = pltpu.get_barrier_semaphore()
    for ahead in range(1, spans):
        pl.semaphore_signal(barrier, inc=1, device_id={"ctx": lax.rem(me + ahead, spans)}, device_id_type=MESH)
    for mask in partners:
        pl.semaphore_signal(barrier, inc=1, device_id={"head": flipped(lane, mask)}, device_id_type=MESH)
    pl.semaphore_wait(barrier, spans - 1 + len(partners))

    def exchange(span, source):
        return pltpu.make_async_remote_copy(
            src_ref=columns(span), dst_ref=xs.at[source, lane],
            send_sem=z_send.at[span], recv_sem=z_recv.at[source],
            device_id={"ctx": span}, device_id_type=MESH,
        )

    def send_rows(outward):
        for distance in range(1, spans):
            for target in (me + distance, me - distance):
                within = (target >= 0) & (target < spans)
                early = edge | ((target > me) == (2 * me > last))

                @pl.when(within & (early if outward else jnp.logical_not(early)))
                def _():
                    exchange(target, me).start()

    def send_aux(side):
        return pltpu.make_async_remote_copy(
            src_ref=aux_own.at[side], dst_ref=aux_all.at[me],
            send_sem=a_send.at[side], recv_sem=a_recv.at[me],
            device_id={"ctx": side * last}, device_id_type=MESH,
        )

    def take_aux(span):
        pltpu.make_async_remote_copy(
            src_ref=aux_own.at[0], dst_ref=aux_all.at[span],
            send_sem=a_send.at[0], recv_sem=a_recv.at[span],
            device_id={"ctx": lax.rem(me + 1, spans)}, device_id_type=MESH,
        ).wait_recv()

    def spread(span, mask):
        block = xs.at[span, lane]
        return pltpu.make_async_remote_copy(
            src_ref=block, dst_ref=block, send_sem=g_send.at[span, mask], recv_sem=g_recv.at[span, mask],
            device_id={"head": flipped(lane, mask)}, device_id_type=MESH,
        )

    def hand_across(span, mask):
        block = xs.at[span, flipped(lane, mask)]
        return pltpu.make_async_remote_copy(
            src_ref=block, dst_ref=block,
            send_sem=g_send.at[span, mask | bits[0]], recv_sem=g_recv.at[span, mask | bits[0]],
            device_id={"head": flipped(lane, bits[0])}, device_id_type=MESH,
        )

    def settled(span, mask):
        block = xs.at[span, flipped(lane, mask)]
        return pltpu.make_async_remote_copy(
            src_ref=block, dst_ref=block, send_sem=g_send.at[span, mask], recv_sem=g_recv.at[span, mask],
            device_id={"head": flipped(lane, bits[0])}, device_id_type=MESH,
        )

    per_place = 2 * per_span
    needed, visits = [], []
    for device in range(spans):
        down = [LAG * (last - device) + per_place * (last - span) for span in range(spans)]
        up = [LAG * device + per_place * span for span in range(spans)]
        when = [min(pair_) for pair_ in zip(down, up)] if sides == 2 else down
        visits.append(sorted(range(spans), key=lambda span: when[span]))
        needed.append(sorted(when))
    needed = [min(device[k] for device in needed) for k in range(spans)]

    def visit(k):
        span = visits[0][k] + 0 * me
        for device in range(1, spans):
            span = jnp.where(me == device, visits[device][k], span)
        return span

    def begin(k):
        span = visit(k)

        @pl.when(me == span)
        def _():
            own.wait()

        @pl.when(me != span)
        def _():
            exchange(span, span).wait_recv()

        for mask in across_chips[1:]:
            spread(span, mask).start()

    def cross(k):
        span = visit(k)
        for mask in across_chips:
            if mask:
                settled(span, mask).wait_recv()
            hand_across(span, mask).start()

    def finish(k):
        span = visit(k)
        for mask in across_chips:
            settled(span, mask | bits[0]).wait_recv()

    def column(span, head):
        return span * aux_all.shape[1] + head

    def prepare():
        aux_all[me] = aux_own[my_side]
        for span in range(spans):

            @pl.when(me != span)
            def _():
                take_aux(span)

        logs = aux_all[...].reshape(spans * aux_all.shape[1], tokens)
        first = lax.broadcasted_iota(jnp.int32, (tokens, tokens), 0)
        second = lax.broadcasted_iota(jnp.int32, (tokens, tokens), 1)
        exact = lax.Precision.HIGHEST
        cum[...] = jnp.dot(
            logs, (first <= second).astype(jnp.float32), precision=exact, preferred_element_type=jnp.float32
        )
        cum_t[...] = lax.dot_general(
            (second <= first).astype(jnp.float32), logs, (((1,), (1,)), ((), ())),
            precision=exact, preferred_element_type=jnp.float32,
        )
        for span in range(spans):
            for head in range(own_heads):
                j = column(span, head)
                down, across = cum_t[:, j : j + 1], cum[j : j + 1, :]
                fade[span, head] = jnp.broadcast_to(jnp.exp(across[:, tokens - 1 :] - down), (tokens, HEAD_DIM))
                reach[span, head] = jnp.broadcast_to(jnp.exp(down), (tokens, HEAD_DIM))
                for a in range(per_span):
                    for e in range(a + 1):
                        level = (a ^ e).bit_length()
                        spread = down[a * BLOCK : (a + 1) * BLOCK, :] - across[:, e * BLOCK : (e + 1) * BLOCK]
                        if e == a:
                            causal = lax.broadcasted_iota(jnp.int32, (BLOCK, BLOCK), 0) >= lax.broadcasted_iota(
                                jnp.int32, (BLOCK, BLOCK), 1
                            )
                            decay = jnp.where(causal, jnp.exp(jnp.where(causal, spread, 0.0)), 0.0)
                        else:
                            decay = jnp.exp(spread)
                        shape[span, head, pair(a, e)] = decay * level_weight(span, a, head, level)

    def level_weight(span, a, head, level):
        held = aux_all[span, own_heads + a : own_heads + a + 1, level : level + 1]
        gain = gain_ref[head : head + 1, level : level + 1]
        if sides == 2:
            other = gain_ref[own_heads + head : own_heads + head + 1, level : level + 1]
            gain = jnp.where(my_side == 0, gain, other)
        return held * gain

    def absorb(place):
        span = jnp.where(my_side == 0, last - place, place)
        at = place * 2 * per_span
        for head in range(own_heads):
            total = None
            for b in range(per_span):
                key = unit(part[my_side, at + b, :, lanes(head)])
                keys[span, head, b] = key
                decayed = (key.astype(jnp.float32) * fade[span, head, b * BLOCK : (b + 1) * BLOCK, :]).astype(jnp.bfloat16)
                term = lax.dot_general(
                    decayed, part[my_side, at + per_span + b, :, lanes(head)], (((0,), (0,)), ((), ())),
                    preferred_element_type=jnp.float32,
                )
                total = term if total is None else total + term
            state[span, head] = total

    def combine():
        for head in range(own_heads):
            totals = [cum[column(s, head) : column(s, head) + 1, tokens - 1 :] for s in range(spans)]
            for span in range(spans):
                carried = {}
                between = jnp.zeros_like(totals[0])
                for e in range(span - 1, -1, -1):
                    m = (span ^ e).bit_length() - 1
                    term = state[e, head] * jnp.exp(between)
                    carried[m] = carried[m] + term if m in carried else term
                    between = between + totals[e]
                for a in range(per_span):
                    mixed = jnp.zeros((HEAD_DIM, HEAD_DIM), jnp.float32)
                    for m, held in carried.items():
                        mixed = mixed + held * level_weight(span, a, head, (2**m * per_span).bit_length())
                    effect[span, a, head] = mixed.astype(jnp.bfloat16)

    def hand_over(span, a):
        return pltpu.make_async_remote_copy(
            src_ref=ho_out.at[span, a], dst_ref=ho.at[my_side, a],
            send_sem=h_send.at[span, a], recv_sem=h_recv.at[my_side, a],
            device_id={"ctx": span}, device_id_type=MESH,
        )

    def take_heads(side, a):
        pltpu.make_async_remote_copy(
            src_ref=ho_out.at[0, a], dst_ref=ho.at[side, a],
            send_sem=h_send.at[0, a], recv_sem=h_recv.at[side, a],
            device_id={"ctx": lax.rem(me + 1, spans)}, device_id_type=MESH,
        ).wait_recv()

    def respond(place, a):
        span = jnp.where(my_side == 0, last - place, place)
        at = place * 2 * per_span + per_span
        for head in range(own_heads):
            query = unit(part[my_side, kv_tiles + place * per_span + a, :, lanes(head)])
            far = (query.astype(jnp.float32) * reach[span, head, a * BLOCK : (a + 1) * BLOCK, :]).astype(jnp.bfloat16)
            result = jnp.dot(far, effect[span, a, head], preferred_element_type=jnp.float32)
            for e in range(a + 1):
                scores = lax.dot_general(
                    query, keys[span, head, e], (((1,), (1,)), ((), ())), preferred_element_type=jnp.float32
                )
                shaped = (scores * shape[span, head, pair(a, e)]).astype(jnp.bfloat16)
                result = result + jnp.dot(
                    shaped, part[my_side, at + e, :, lanes(head)], preferred_element_type=jnp.float32
                )
            ho_out[span, a, :, lanes(head)] = result.astype(jnp.bfloat16)

        @pl.when(span == me)
        def _():
            ho[my_side, a] = ho_out[span, a]

        @pl.when(span != me)
        def _():
            hand_over(span, a).start()

    def attend(i):
        place = i // (2 * per_span)

        @pl.when((i < kv_tiles) & (i % (2 * per_span) == 2 * per_span - 1))
        def _():
            absorb(place)

        pl.when(i == kv_tiles - 1)(combine)
        for a in range(per_span):

            @pl.when((i >= kv_tiles) & (i % per_span == a))
            def _():
                respond((i - kv_tiles) // per_span, a)

    def link(side, i):
        step = jnp.where(side == 0, -1, 1)
        return pltpu.make_async_remote_copy(
            src_ref=part.at[side, i], dst_ref=inbox.at[side, i],
            send_sem=p_send.at[side, i], recv_sem=p_recv.at[side, i],
            device_id={"ctx": lax.rem(me + step + spans, spans)}, device_id_type=MESH,
        )

    def place_in_chain(side):
        return jnp.where(side == 0, last - me, me)

    def add_tile(side, t, may_own):
        p = place_in_chain(side)
        i = t - LAG * p

        @pl.when((i >= 0) & (i < tiles))
        def _():
            late = i >= kv_tiles
            pos = jnp.where(late, (i - kv_tiles) // per_span, i // (2 * per_span))
            kind = jnp.where(late, 0, 1 + (i % (2 * per_span)) // per_span)
            span = jnp.where(side == 0, last - pos, pos)
            block = xs[span, pl.ds((i % per_span) * blocks_of_rows, blocks_of_rows)]
            if rows % 16:
                block = block.astype(jnp.float32)
            block = block.reshape(BLOCK, depth).astype(jnp.bfloat16)
            product = jnp.dot(block, weight[side, kind], preferred_element_type=jnp.float32)

            @pl.when(p == 0)
            def _():
                part[side, i] = product.astype(jnp.bfloat16)

            @pl.when(p > 0)
            def _():
                link(side, i).wait_recv()
                part[side, i] = (product + inbox[side, i].astype(jnp.float32)).astype(jnp.bfloat16)

            @pl.when(p < last)
            def _():
                link(side, i).start()

            if may_own:

                @pl.when(p == last)
                def _():
                    attend(i)

    if sides == 2:
        first_side = jnp.where(me < last - me, 1, 0)
        order = [first_side, 1 - first_side]
    else:
        order = [0]

    def steps(start, stop):
        def body(t, carry):
            for which, side in enumerate(order):
                add_tile(side, t, which == sides - 1 and stop > LAG * last)
            return carry

        lax.fori_loop(start, stop, body, 0)

    send_rows(True)
    events = {}
    for k in range(spans):
        at = max(needed[k] - 2, 0) if k else -1
        events.setdefault(at, []).append((1, k))
        events.setdefault(max(needed[k], 0) if k else -1, []).append((2, k))
        events.setdefault(-1 if k < 3 else max(needed[k - 2] - 2, 0), []).append((0, k))
    for load in small_loads:
        load.wait()
    begin(0)
    if spans > 1:
        begin(1)
    send_rows(False)
    cross(0)
    if spans > 2:
        begin(2)
    aux_own[...] = jnp.zeros_like(aux_own)
    for side in range(sides):
        aux_own[side, :own_heads, :] = decay_ref[side * own_heads : (side + 1) * own_heads, :]
        aux_own[side, own_heads : own_heads + per_span, : mask_ref.shape[1]] = mask_ref[...].astype(jnp.float32)
    for side in range(sides):

        @pl.when(me != side * last)
        def _():
            send_aux(side).start()

    for load in loads:
        load.wait()
    finish(0)
    done, act = 0, (begin, cross, finish, lambda _: pl.when(owner)(prepare))
    events.setdefault(LAG * last, []).append((3, 0))
    for at in sorted(key for key in events if key >= 0):
        if at > done:
            steps(done, at)
            done = at
        for action, k in sorted(events[at], key=lambda event: -event[0] % 4):
            act[action](k)
    for load in out_loads:
        load.start()
    steps(done, tiles + LAG * last)

    for a in range(per_span):
        for side in range(sides):

            @pl.when(me != side * last)
            def _():
                take_heads(side, a)

    orders = [bits[:1] + bits[1:], bits[:1] + bits[:0:-1]]

    def transfer(j, phase, mask):
        bit = orders[j % 2][phase]
        return pltpu.make_async_remote_copy(
            src_ref=share.at[j, flipped(lane, mask | bit)], dst_ref=arrived.at[j, phase, mask],
            send_sem=s_send.at[j, phase, mask], recv_sem=s_recv.at[j, phase, mask],
            device_id={"head": flipped(lane, bit)}, device_id_type=MESH,
        )

    def advance(j, phase):
        path = orders[j % 2]
        if phase == 0:
            out_loads[j].wait()
            product = None
            for side in range(sides):
                term = jnp.dot(
                    ho[side].reshape(tokens, width), w_out[j, side * width : (side + 1) * width, :],
                    preferred_element_type=jnp.float32,
                )
                product = term if product is None else product + term
            share[j] = product.reshape(heads, rows, chunk).astype(jnp.bfloat16)
        else:
            for mask in subsets(path[phase:]):
                transfer(j, phase - 1, mask).wait_recv()
                place = flipped(lane, mask)
                added = share[j, place].astype(jnp.float32) + arrived[j, phase - 1, mask].astype(jnp.float32)
                if phase < len(bits):
                    share[j, place] = added.astype(jnp.bfloat16)
                else:
                    out_ref[:, pl.ds(j * chunk, chunk)] = added.astype(jnp.bfloat16)
        if phase < len(bits):
            for mask in subsets(path[phase + 1 :]):
                transfer(j, phase, mask).start()

    for phase in range(len(bits) + 1):
        for j in range(chunks):
            advance(j, phase)

    for j in range(chunks):
        for phase in range(len(bits)):
            for mask in subsets(orders[j % 2][phase + 1 :]):
                transfer(j, phase, mask).wait_send()
    for distance in range(1, spans):
        exchange(lax.rem(me + distance, spans), me).wait_send()
    for span in range(spans):
        for mask in range(1, heads):
            settled(span, mask).wait_send()
    for side in range(sides):

        @pl.when(me != side * last)
        def _():
            send_aux(side).wait_send()

        @pl.when(place_in_chain(side) < last)
        def _():
            def drain(i, carry):
                link(side, i).wait_send()
                return carry

            lax.fori_loop(0, tiles, drain, 0)

    for span in range(spans):
        for a in range(per_span):

            @pl.when(owner & (me != span))
            def _():
                hand_over(span, a).wait_send()


def on_device(layer_input, w_query, w_key, w_value, w_out, log_decay, level_gain, level_mask):
    spans, heads = lax.axis_size("ctx"), lax.axis_size("head")
    rows, model = layer_input.shape
    depth, columns = w_query.shape
    local_heads, tokens = log_decay.shape
    sides = 2 if local_heads % 2 == 0 and spans > 1 else 1
    width = columns // sides
    own_heads = local_heads // sides
    per_span = tokens // BLOCK
    tiles = 3 * per_span * spans
    aux_rows = -(-(own_heads + per_span) // 8) * 8
    pairs = per_span * (per_span + 1) // 2
    chunk = model // CHUNKS
    phases = heads.bit_length() - 1
    dma = pltpu.SemaphoreType.DMA
    hbm = pl.BlockSpec(memory_space=pl.ANY)
    vmem = pl.BlockSpec(memory_space=pltpu.VMEM)
    half, full = jnp.bfloat16, jnp.float32
    return pl.pallas_call(
        functools.partial(layer_kernel, spans, heads),
        out_shape=jax.ShapeDtypeStruct((rows, model), half),
        in_specs=[hbm] * 8,
        out_specs=vmem,
        scratch_shapes=[
            pltpu.VMEM(log_decay.shape, log_decay.dtype),
            pltpu.VMEM(level_gain.shape, level_gain.dtype),
            pltpu.VMEM(level_mask.shape, level_mask.dtype),
            pltpu.VMEM((spans, heads, rows, depth), half),
            pltpu.VMEM((sides, 3, depth, width), half),
            pltpu.VMEM((sides, tiles, BLOCK, width), half),
            pltpu.VMEM((sides, tiles, BLOCK, width), half),
            pltpu.VMEM((sides, aux_rows, tokens), full),
            pltpu.VMEM((spans, aux_rows, tokens), full),
            pltpu.VMEM((spans * aux_rows, tokens), full),
            pltpu.VMEM((tokens, spans * aux_rows), full),
            pltpu.VMEM((spans, own_heads, pairs, BLOCK, BLOCK), full),
            pltpu.VMEM((spans, own_heads, tokens, HEAD_DIM), full),
            pltpu.VMEM((spans, own_heads, tokens, HEAD_DIM), full),
            pltpu.VMEM((spans, own_heads, per_span, BLOCK, HEAD_DIM), half),
            pltpu.VMEM((spans, own_heads, HEAD_DIM, HEAD_DIM), full),
            pltpu.VMEM((spans, per_span, own_heads, HEAD_DIM, HEAD_DIM), half),
            pltpu.VMEM((spans, per_span, BLOCK, width), half),
            pltpu.VMEM((sides, per_span, BLOCK, width), half),
            pltpu.VMEM((CHUNKS, columns, chunk), half),
            pltpu.VMEM((CHUNKS, heads, rows, chunk), half),
            pltpu.VMEM((CHUNKS, phases, heads, rows, chunk), half),
            dma((3,)), dma((sides, 3)), dma((CHUNKS,)), dma((spans,)), dma((spans,)), dma,
            dma((spans, heads)), dma((spans, heads)),
            dma((sides, tiles)), dma((sides, tiles)),
            dma((sides,)), dma((spans,)),
            dma((spans, per_span)), dma((sides, per_span)),
            dma((CHUNKS, phases, heads)), dma((CHUNKS, phases, heads)),
        ],
        compiler_params=pltpu.CompilerParams(collective_id=0, has_side_effects=True, vmem_limit_bytes=VMEM_LIMIT),
        name="layer",
    )(layer_input, w_query, w_key, w_value, w_out, log_decay, level_gain, level_mask)


def solution(mesh):
    in_specs = (
        P(("ctx", "head"), None),
        P("ctx", "head"),
        P("ctx", "head"),
        P("ctx", "head"),
        P("head", None),
        P("head", "ctx"),
        P("head", None),
        P("ctx", None),
    )
    out_specs = P(("ctx", "head"), None)
    return jax.shard_map(
        on_device, mesh=mesh, in_specs=in_specs, out_specs=out_specs, check_vma=False
    )
```

```python
import functools

import jax
import jax.numpy as jnp
from jax import lax
from jax.experimental import pallas as pl
from jax.experimental.pallas import tpu as pltpu
from jax.sharding import PartitionSpec as P

HEAD_DIM = 128
BLOCK = 128
LAG = 5
AFTER = 3
PAUSE = 2
CHUNKS = 4
VMEM_LIMIT = 60 * 2**20
MESH = pl.DeviceIdType.MESH


def flipped(index, mask):
    bit = 1
    while bit <= mask:
        if mask & bit:
            index = index + bit - 2 * bit * ((index // bit) % 2)
        bit *= 2
    return index


def subsets(bits):
    masks = [0]
    for bit in bits:
        masks = masks + [mask | bit for mask in masks]
    return masks


def bits_of(count):
    return [2**k for k in range(count.bit_length() - 1)]


def exclusive(first, second, count):
    result = 0
    for bit in bits_of(count):
        x, y = (first // bit) % 2, (second // bit) % 2
        result = result + (x + y - 2 * x * y) * bit
    return result


def unit(block):
    floated = block.astype(jnp.float32)
    return (floated * lax.rsqrt(jnp.sum(floated * floated, axis=-1, keepdims=True) + 1e-06)).astype(jnp.bfloat16)


def lanes(head):
    return slice(head * HEAD_DIM, (head + 1) * HEAD_DIM)


def layer_kernel(
    spans, heads, x_ref, wq_ref, wk_ref, wv_ref, w_out_ref, decay_in, gain_in, mask_in, out_ref,
    decay_ref, gain_ref, mask_ref,
    xs, weight, part, inbox, aux_own, aux_all, cum, cum_t, shape, fade, reach, keys, state, effect,
    ho_out, ho, w_out, share, beside, arrived,
    small_sem, w_sem, wo_sem, z_send, z_recv, own_sem, g_send, g_recv, p_send, p_recv, a_send, a_recv, h_send, h_recv, b_send, b_recv, s_send, s_recv,
):
    me, lane = lax.axis_index("ctx"), lax.axis_index("head")
    rows = x_ref.shape[0]
    sides, _, depth, width = weight.shape
    own_heads = width // HEAD_DIM
    tokens = heads * rows
    per_span = tokens // BLOCK
    chips = heads // 2
    chip, core = lane // 2, lane % 2
    tile_rows = 2 * rows
    per_block = BLOCK // tile_rows
    tiles, kv_tiles = 3 * chips * spans, 2 * chips * spans
    chunks, chunk = CHUNKS, w_out.shape[-1]
    bits = bits_of(heads)
    across_chips = subsets(bits[1:])
    partners = across_chips[1:] + bits[:1]
    last = spans - 1
    edge = (me == 0) | (me == last)
    my_side = jnp.where(me == 0, 0, sides - 1)
    owner = edge if sides == 2 else me == 0

    def columns(span):
        return x_ref.at[:, pl.ds(pl.multiple_of(span * depth, depth), depth)]

    own = pltpu.make_async_copy(columns(me), xs.at[me, lane], own_sem)
    own.start()
    loads = [
        pltpu.make_async_copy(ref.at[:, pl.ds(side * width, width)], weight.at[side, k], w_sem.at[side, k])
        for k, ref in ((1, wk_ref), (2, wv_ref), (0, wq_ref))
        for side in range(sides)
    ]
    out_loads = [
        pltpu.make_async_copy(w_out_ref.at[:, pl.ds(j * chunk, chunk)], w_out.at[j], wo_sem.at[j]) for j in range(chunks)
    ]
    small_loads = [
        pltpu.make_async_copy(source, target, small_sem.at[k])
        for k, (source, target) in enumerate(((decay_in, decay_ref), (gain_in, gain_ref), (mask_in, mask_ref)))
    ]
    for load in loads + small_loads:
        load.start()

    barrier = pltpu.get_barrier_semaphore()
    for ahead in range(1, spans):
        pl.semaphore_signal(barrier, inc=1, device_id={"ctx": lax.rem(me + ahead, spans)}, device_id_type=MESH)
    for mask in partners:
        pl.semaphore_signal(barrier, inc=1, device_id={"head": flipped(lane, mask)}, device_id_type=MESH)
    pl.semaphore_wait(barrier, spans - 1 + len(partners))

    def exchange(span, source):
        return pltpu.make_async_remote_copy(
            src_ref=columns(span), dst_ref=xs.at[source, lane],
            send_sem=z_send.at[span], recv_sem=z_recv.at[source],
            device_id={"ctx": span}, device_id_type=MESH,
        )

    def send_rows(outward):
        for distance in range(1, spans):
            for target in (me + distance, me - distance):
                within = (target >= 0) & (target < spans)
                early = edge | ((target > me) == (2 * me > last))

                @pl.when(within & (early if outward else jnp.logical_not(early)))
                def _():
                    exchange(target, me).start()

    def send_aux(side):
        return pltpu.make_async_remote_copy(
            src_ref=aux_own.at[side], dst_ref=aux_all.at[me],
            send_sem=a_send.at[side], recv_sem=a_recv.at[me],
            device_id={"ctx": side * last}, device_id_type=MESH,
        )

    def take_aux(span):
        pltpu.make_async_remote_copy(
            src_ref=aux_own.at[0], dst_ref=aux_all.at[span],
            send_sem=a_send.at[0], recv_sem=a_recv.at[span],
            device_id={"ctx": lax.rem(me + 1, spans)}, device_id_type=MESH,
        ).wait_recv()

    def spread(span, mask):
        block = xs.at[span, lane]
        return pltpu.make_async_remote_copy(
            src_ref=block, dst_ref=block, send_sem=g_send.at[span, mask], recv_sem=g_recv.at[span, mask],
            device_id={"head": flipped(lane, mask)}, device_id_type=MESH,
        )

    def hand_across(span, mask):
        block = xs.at[span, flipped(lane, mask)]
        return pltpu.make_async_remote_copy(
            src_ref=block, dst_ref=block,
            send_sem=g_send.at[span, mask | bits[0]], recv_sem=g_recv.at[span, mask | bits[0]],
            device_id={"head": flipped(lane, bits[0])}, device_id_type=MESH,
        )

    def settled(span, mask):
        block = xs.at[span, flipped(lane, mask)]
        return pltpu.make_async_remote_copy(
            src_ref=block, dst_ref=block, send_sem=g_send.at[span, mask], recv_sem=g_recv.at[span, mask],
            device_id={"head": flipped(lane, bits[0])}, device_id_type=MESH,
        )

    per_place = 2 * chips
    needed, visits = [], []
    for device in range(spans):
        down = [LAG * (last - device) + per_place * (last - span) for span in range(spans)]
        up = [LAG * device + per_place * span for span in range(spans)]
        when = [min(pair_) for pair_ in zip(down, up)] if sides == 2 else down
        visits.append(sorted(range(spans), key=lambda span: when[span]))
        needed.append(sorted(when))
    needed = [min(device[k] for device in needed) for k in range(spans)]

    def visit(k):
        span = visits[0][k] + 0 * me
        for device in range(1, spans):
            span = jnp.where(me == device, visits[device][k], span)
        return span

    def begin(k):
        span = visit(k)

        @pl.when(me == span)
        def _():
            own.wait()

        @pl.when(me != span)
        def _():
            exchange(span, span).wait_recv()

        for mask in across_chips[1:]:
            spread(span, mask).start()

    def cross(k):
        span = visit(k)
        for mask in across_chips:
            if mask:
                settled(span, mask).wait_recv()
            hand_across(span, mask).start()

    def finish(k):
        span = visit(k)
        for mask in across_chips:
            settled(span, mask | bits[0]).wait_recv()

    def column(span, head):
        return span * aux_all.shape[1] + head

    def prepare():
        aux_all[me] = aux_own[my_side]
        for span in range(spans):

            @pl.when(me != span)
            def _():
                take_aux(span)

        logs = aux_all[...].reshape(spans * aux_all.shape[1], tokens)
        first = lax.broadcasted_iota(jnp.int32, (tokens, tokens), 0)
        second = lax.broadcasted_iota(jnp.int32, (tokens, tokens), 1)
        exact = lax.Precision.HIGHEST
        cum[...] = jnp.dot(
            logs, (first <= second).astype(jnp.float32), precision=exact, preferred_element_type=jnp.float32
        )
        cum_t[...] = lax.dot_general(
            (second <= first).astype(jnp.float32), logs, (((1,), (1,)), ((), ())),
            precision=exact, preferred_element_type=jnp.float32,
        )
        for span in range(spans):
            for head in range(own_heads):
                j = column(span, head)
                down, across = cum_t[:, j : j + 1], cum[j : j + 1, :]
                fade[span, head] = jnp.broadcast_to(jnp.exp(across[:, tokens - 1 :] - down), (tokens, HEAD_DIM))
                reach[span, head] = jnp.broadcast_to(jnp.exp(down), (tokens, HEAD_DIM))
                for a in range(per_span):
                    for e in range(per_span):
                        at = slice(a * BLOCK, (a + 1) * BLOCK), slice(e * BLOCK, (e + 1) * BLOCK)
                        if e > a:
                            shape[span, head, at[0], at[1]] = jnp.zeros((BLOCK, BLOCK), jnp.float32)
                            continue
                        level = (a ^ e).bit_length()
                        spread = down[at[0], :] - across[:, at[1]]
                        if e == a:
                            causal = lax.broadcasted_iota(jnp.int32, (BLOCK, BLOCK), 0) >= lax.broadcasted_iota(
                                jnp.int32, (BLOCK, BLOCK), 1
                            )
                            decay = jnp.where(causal, jnp.exp(jnp.where(causal, spread, 0.0)), 0.0)
                        else:
                            decay = jnp.exp(spread)
                        shape[span, head, at[0], at[1]] = decay * level_weight(span, a, head, level)

    def level_weight(span, a, head, level):
        held = aux_all[span, own_heads + a : own_heads + a + 1, level : level + 1]
        gain = gain_ref[head : head + 1, level : level + 1]
        if sides == 2:
            other = gain_ref[own_heads + head : own_heads + head + 1, level : level + 1]
            gain = jnp.where(my_side == 0, gain, other)
        return held * gain

    def absorb(place):
        span = jnp.where(my_side == 0, last - place, place)
        for head in range(own_heads):
            key = unit(part[my_side, 1, span, :, :, lanes(head)].reshape(tokens, HEAD_DIM))
            keys[span, head] = key
            decayed = (key.astype(jnp.float32) * fade[span, head]).astype(jnp.bfloat16)
            value = part[my_side, 2, span, :, :, lanes(head)].reshape(tokens, HEAD_DIM)
            state[span, head] = lax.dot_general(
                decayed, value, (((0,), (0,)), ((), ())), preferred_element_type=jnp.float32
            )

    def combine():
        for head in range(own_heads):
            totals = [cum[column(s, head) : column(s, head) + 1, tokens - 1 :] for s in range(spans)]
            for span in range(spans):
                carried = {}
                between = jnp.zeros_like(totals[0])
                for e in range(span - 1, -1, -1):
                    m = (span ^ e).bit_length() - 1
                    term = state[e, head] * jnp.exp(between)
                    carried[m] = carried[m] + term if m in carried else term
                    between = between + totals[e]
                for a in range(per_span):
                    mixed = jnp.zeros((HEAD_DIM, HEAD_DIM), jnp.float32)
                    for m, held in carried.items():
                        mixed = mixed + held * level_weight(span, a, head, (2**m * per_span).bit_length())
                    effect[span, a, head] = mixed.astype(jnp.bfloat16)

    def hand_over(span, d):
        return pltpu.make_async_remote_copy(
            src_ref=ho_out.at[span, d], dst_ref=ho.at[my_side, d],
            send_sem=h_send.at[span, d], recv_sem=h_recv.at[my_side, d],
            device_id={"ctx": span}, device_id_type=MESH,
        )

    def take_heads(side, d):
        pltpu.make_async_remote_copy(
            src_ref=ho_out.at[0, d], dst_ref=ho.at[side, d],
            send_sem=h_send.at[0, d], recv_sem=h_recv.at[side, d],
            device_id={"ctx": lax.rem(me + 1, spans)}, device_id_type=MESH,
        ).wait_recv()

    def respond(span, d):
        inside = pl.ds(pl.multiple_of(d * tile_rows, tile_rows), tile_rows)
        query = [unit(part[my_side, 0, span, d, :, lanes(head)]) for head in range(own_heads)]
        scores = [
            lax.dot_general(
                query[head], keys[span, head], (((1,), (1,)), ((), ())), preferred_element_type=jnp.float32
            )
            for head in range(own_heads)
        ]
        far = [
            jnp.dot(
                (query[head].astype(jnp.float32) * reach[span, head, inside, :]).astype(jnp.bfloat16),
                effect[span, d // per_block, head], preferred_element_type=jnp.float32,
            )
            for head in range(own_heads)
        ]
        shaped = [(scores[head] * shape[span, head, inside, :]).astype(jnp.bfloat16) for head in range(own_heads)]
        for head in range(own_heads):
            value = part[my_side, 2, span, :, :, lanes(head)].reshape(tokens, HEAD_DIM)
            near = jnp.dot(shaped[head], value, preferred_element_type=jnp.float32)
            ho_out[span, d, :, lanes(head)] = (near + far[head]).astype(jnp.bfloat16)

        @pl.when(span == me)
        def _():
            ho[my_side, d] = ho_out[span, d]

        @pl.when(span != me)
        def _():
            hand_over(span, d).start()

    def attend(i, span, d):
        @pl.when((i < kv_tiles) & (i % per_place == per_place - 1))
        def _():
            absorb(i // per_place)

        pl.when(i == kv_tiles - 1)(combine)

        @pl.when(i >= kv_tiles)
        def _():
            respond(span, d)

    def link(side, kind, span, d):
        step = jnp.where(side == 0, -1, 1)
        k = (kind * spans + span) * chips + d
        return pltpu.make_async_remote_copy(
            src_ref=part.at[side, kind, span, d], dst_ref=inbox.at[side, kind, span, d],
            send_sem=p_send.at[side, k], recv_sem=p_recv.at[side, k],
            device_id={"ctx": lax.rem(me + step + spans, spans)}, device_id_type=MESH,
        )

    def place_in_chain(side):
        return jnp.where(side == 0, last - me, me)

    def add_tile(side, t, may_own):
        p = place_in_chain(side)
        i = t - LAG * p

        @pl.when((i >= 0) & (i < tiles))
        def _():
            late = i >= kv_tiles
            pos = jnp.where(late, (i - kv_tiles) % spans, i // per_place)
            kind = jnp.where(late, 0, 1 + (i % per_place) // chips)
            span = jnp.where(side == 0, last - pos, pos)
            d = exclusive(chip, jnp.where(late, chips - 1 - (i - kv_tiles) // spans, i % chips), chips)
            block = xs[span, pl.ds(2 * d, 2)]
            if rows % 16:
                block = block.astype(jnp.float32)
            block = block.reshape(tile_rows, depth).astype(jnp.bfloat16)
            product = jnp.dot(block, weight[side, kind], preferred_element_type=jnp.float32)

            @pl.when(p == 0)
            def _():
                part[side, kind, span, d] = product.astype(jnp.bfloat16)

            @pl.when(p > 0)
            def _():
                link(side, kind, span, d).wait_recv()
                added = product + inbox[side, kind, span, d].astype(jnp.float32)
                part[side, kind, span, d] = added.astype(jnp.bfloat16)

            @pl.when(p < last)
            def _():
                link(side, kind, span, d).start()

            if may_own:

                @pl.when(p == last)
                def _():
                    attend(i, span, d)

    def to_sibling(j):
        return pltpu.make_async_remote_copy(
            src_ref=share.at[j, 1 - core], dst_ref=beside.at[j],
            send_sem=b_send.at[j], recv_sem=b_recv.at[j],
            device_id={"head": flipped(lane, 1)}, device_id_type=MESH,
        )

    def to_owner(j):
        return pltpu.make_async_remote_copy(
            src_ref=share.at[j, core], dst_ref=arrived.at[j],
            send_sem=s_send.at[j], recv_sem=s_recv.at[j],
            device_id={"head": 2 * exclusive(chip, j, chips) + core}, device_id_type=MESH,
        )

    def emit(j):
        d = exclusive(chip, j, chips)
        for side in range(sides):

            @pl.when(me != side * last)
            def _():
                take_heads(side, d)

        for c in range(chunks):
            product = None
            for side in range(sides):
                term = jnp.dot(
                    ho[side, d], w_out[c, side * width : (side + 1) * width, :], preferred_element_type=jnp.float32
                )
                product = term if product is None else product + term
            for k in range(2):
                share[j, k, :, c * chunk : (c + 1) * chunk] = product[k * rows : (k + 1) * rows, :].astype(jnp.bfloat16)
        to_sibling(j).start()

    def settle(j):
        to_sibling(j).wait_recv()
        for c in range(chunks):
            at = slice(c * chunk, (c + 1) * chunk)
            added = share[j, core, :, at].astype(jnp.float32) + beside[j, :, at].astype(jnp.float32)
            share[j, core, :, at] = added.astype(jnp.bfloat16)

        @pl.when(j > 0)
        def _():
            to_owner(j).start()

    first_out = kv_tiles + LAG * last + last + AFTER
    end = first_out + spans * (chips - 1) + PAUSE + 1

    def give(t):
        for offset, act in ((0, emit), (PAUSE, settle)):
            after = t - first_out - offset

            @pl.when((after >= 0) & (after % spans == 0) & (after < spans * chips))
            def _():
                act(chips - 1 - after // spans)

    if sides == 2:
        first_side = jnp.where(me < last - me, 1, 0)
        order = [first_side, 1 - first_side]
    else:
        order = [0]

    def steps(start, stop):
        def body(t, carry):
            for which, side in enumerate(order):
                add_tile(side, t, which == sides - 1 and stop > LAG * last)
            if stop > first_out:
                give(t)
            return carry

        lax.fori_loop(start, stop, body, 0)

    send_rows(True)
    events = {}
    for k in range(spans):
        at = max(needed[k] - 2, 0) if k else -1
        events.setdefault(at, []).append((1, k))
        events.setdefault(max(needed[k], 0) if k else -1, []).append((2, k))
        events.setdefault(-1 if k < 3 else max(needed[k - 2] - 2, 0), []).append((0, k))
    for load in small_loads:
        load.wait()
    begin(0)
    if spans > 1:
        begin(1)
    send_rows(False)
    cross(0)
    if spans > 2:
        begin(2)
    aux_own[...] = jnp.zeros_like(aux_own)
    for side in range(sides):
        aux_own[side, :own_heads, :] = decay_ref[side * own_heads : (side + 1) * own_heads, :]
        aux_own[side, own_heads : own_heads + per_span, : mask_ref.shape[1]] = mask_ref[...].astype(jnp.float32)
    for side in range(sides):

        @pl.when(me != side * last)
        def _():
            send_aux(side).start()

    for load in loads:
        load.wait()
    for load in out_loads:
        load.start()
    finish(0)
    done, act = 0, (begin, cross, finish, lambda _: pl.when(owner)(prepare))
    events.setdefault(LAG * last, []).append((3, 0))
    for at in sorted(key for key in events if key >= 0):
        if at > done:
            steps(done, at)
            done = at
        for action, k in sorted(events[at], key=lambda event: -event[0] % 4):
            act[action](k)
    steps(done, LAG * last + per_place)
    for load in out_loads:
        load.wait()
    steps(LAG * last + per_place, end)
    for c in range(chunks):
        at = slice(c * chunk, (c + 1) * chunk)
        added = share[0, core, :, at].astype(jnp.float32)
        for j in range(chips - 1, 0, -1):
            if c == 0:
                to_owner(j).wait_recv()
            added = added + arrived[j, :, at].astype(jnp.float32)
        out_ref[:, at] = added.astype(jnp.bfloat16)

    for j in range(chips):
        to_sibling(j).wait_send()
        if j:
            to_owner(j).wait_send()
    for distance in range(1, spans):
        exchange(lax.rem(me + distance, spans), me).wait_send()
    for span in range(spans):
        for mask in range(1, heads):
            settled(span, mask).wait_send()
    for side in range(sides):

        @pl.when(me != side * last)
        def _():
            send_aux(side).wait_send()

        @pl.when(place_in_chain(side) < last)
        def _():
            def drain(i, carry):
                link(side, i // (chips * spans), (i // chips) % spans, i % chips).wait_send()
                return carry

            lax.fori_loop(0, tiles, drain, 0)

    for span in range(spans):
        for d in range(chips):

            @pl.when(owner & (me != span))
            def _():
                hand_over(span, d).wait_send()


def on_device(layer_input, w_query, w_key, w_value, w_out, log_decay, level_gain, level_mask):
    spans, heads = lax.axis_size("ctx"), lax.axis_size("head")
    rows, model = layer_input.shape
    depth, columns = w_query.shape
    local_heads, tokens = log_decay.shape
    sides = 2 if local_heads % 2 == 0 and spans > 1 else 1
    width = columns // sides
    own_heads = local_heads // sides
    per_span = tokens // BLOCK
    chips, tile_rows = heads // 2, 2 * rows
    tiles = 3 * chips * spans
    aux_rows = -(-(own_heads + per_span) // 8) * 8
    chunk = model // CHUNKS
    dma = pltpu.SemaphoreType.DMA
    hbm = pl.BlockSpec(memory_space=pl.ANY)
    vmem = pl.BlockSpec(memory_space=pltpu.VMEM)
    half, full = jnp.bfloat16, jnp.float32
    return pl.pallas_call(
        functools.partial(layer_kernel, spans, heads),
        out_shape=jax.ShapeDtypeStruct((rows, model), half),
        in_specs=[hbm] * 8,
        out_specs=vmem,
        scratch_shapes=[
            pltpu.VMEM(log_decay.shape, log_decay.dtype),
            pltpu.VMEM(level_gain.shape, level_gain.dtype),
            pltpu.VMEM(level_mask.shape, level_mask.dtype),
            pltpu.VMEM((spans, heads, rows, depth), half),
            pltpu.VMEM((sides, 3, depth, width), half),
            pltpu.VMEM((sides, 3, spans, chips, tile_rows, width), half),
            pltpu.VMEM((sides, 3, spans, chips, tile_rows, width), half),
            pltpu.VMEM((sides, aux_rows, tokens), full),
            pltpu.VMEM((spans, aux_rows, tokens), full),
            pltpu.VMEM((spans * aux_rows, tokens), full),
            pltpu.VMEM((tokens, spans * aux_rows), full),
            pltpu.VMEM((spans, own_heads, tokens, tokens), full),
            pltpu.VMEM((spans, own_heads, tokens, HEAD_DIM), full),
            pltpu.VMEM((spans, own_heads, tokens, HEAD_DIM), full),
            pltpu.VMEM((spans, own_heads, tokens, HEAD_DIM), half),
            pltpu.VMEM((spans, own_heads, HEAD_DIM, HEAD_DIM), full),
            pltpu.VMEM((spans, per_span, own_heads, HEAD_DIM, HEAD_DIM), half),
            pltpu.VMEM((spans, chips, tile_rows, width), half),
            pltpu.VMEM((sides, chips, tile_rows, width), half),
            pltpu.VMEM((CHUNKS, columns, chunk), half),
            pltpu.VMEM((chips, 2, rows, model), half),
            pltpu.VMEM((chips, rows, model), half),
            pltpu.VMEM((chips, rows, model), half),
            dma((3,)), dma((sides, 3)), dma((CHUNKS,)), dma((spans,)), dma((spans,)), dma,
            dma((spans, heads)), dma((spans, heads)),
            dma((sides, tiles)), dma((sides, tiles)),
            dma((sides,)), dma((spans,)),
            dma((spans, chips)), dma((sides, chips)),
            dma((chips,)), dma((chips,)), dma((chips,)), dma((chips,)),
        ],
        compiler_params=pltpu.CompilerParams(collective_id=0, has_side_effects=True, vmem_limit_bytes=VMEM_LIMIT),
        name="layer",
    )(layer_input, w_query, w_key, w_value, w_out, log_decay, level_gain, level_mask)


def solution(mesh):
    in_specs = (
        P(("ctx", "head"), None),
        P("ctx", "head"),
        P("ctx", "head"),
        P("ctx", "head"),
        P("head", None),
        P("head", "ctx"),
        P("head", None),
        P("ctx", None),
    )
    out_specs = P(("ctx", "head"), None)
    return jax.shard_map(
        on_device, mesh=mesh, in_specs=in_specs, out_specs=out_specs, check_vma=False
    )
```

```python
import functools

import jax
import jax.numpy as jnp
from jax import lax
from jax.experimental import pallas as pl
from jax.experimental.pallas import tpu as pltpu
from jax.sharding import PartitionSpec as P

HEAD_DIM = 128
BLOCK = 128
LAG = 5
AFTER = 3
PAUSE = 2
KEPT = 5
CHUNKS = 4
VMEM_LIMIT = 60 * 2**20
MESH = pl.DeviceIdType.MESH


def flipped(index, mask):
    bit = 1
    while bit <= mask:
        if mask & bit:
            index = index + bit - 2 * bit * ((index // bit) % 2)
        bit *= 2
    return index


def subsets(bits):
    masks = [0]
    for bit in bits:
        masks = masks + [mask | bit for mask in masks]
    return masks


def bits_of(count):
    return [2**k for k in range(count.bit_length() - 1)]


def exclusive(first, second, count):
    result = 0
    for bit in bits_of(count):
        x, y = (first // bit) % 2, (second // bit) % 2
        result = result + (x + y - 2 * x * y) * bit
    return result


def unit(block):
    floated = block.astype(jnp.float32)
    return (floated * lax.rsqrt(jnp.sum(floated * floated, axis=-1, keepdims=True) + 1e-06)).astype(jnp.bfloat16)


def lanes(head):
    return slice(head * HEAD_DIM, (head + 1) * HEAD_DIM)


def layer_kernel(
    spans, heads, x_ref, wq_ref, wk_ref, wv_ref, w_out_ref, decay_in, gain_in, mask_in, out_ref,
    decay_ref, gain_ref, mask_ref,
    xs, weight, part, inbox, aux_own, aux_all, cum, cum_t, shape, fade, reach, keys, state, effect,
    ho_out, ho, w_out, share, beside, arrived,
    small_sem, w_sem, wo_sem, z_send, z_recv, own_sem, g_send, g_recv, p_send, p_recv, a_send, a_recv, h_send, h_recv, b_send, b_recv, s_send, s_recv,
):
    me, lane = lax.axis_index("ctx"), lax.axis_index("head")
    rows = x_ref.shape[0]
    sides, _, depth, width = weight.shape
    own_heads = width // HEAD_DIM
    tokens = heads * rows
    per_span = tokens // BLOCK
    chips = heads // 2
    chip, core = lane // 2, lane % 2
    tile_rows = 2 * rows
    per_block = BLOCK // tile_rows
    tiles, kv_tiles = 3 * chips * spans, 2 * chips * spans
    chunks, chunk = CHUNKS, w_out.shape[-1]
    bits = bits_of(heads)
    across_chips = subsets(bits[1:])
    partners = across_chips[1:] + bits[:1]
    last = spans - 1
    edge = (me == 0) | (me == last)
    my_side = jnp.where(me == 0, 0, sides - 1)
    owner = edge if sides == 2 else me == 0

    def columns(span):
        return x_ref.at[:, pl.ds(pl.multiple_of(span * depth, depth), depth)]

    own = pltpu.make_async_copy(columns(me), xs.at[me, lane], own_sem)
    own.start()
    loads = [
        pltpu.make_async_copy(ref.at[:, pl.ds(side * width, width)], weight.at[side, k], w_sem.at[side, k])
        for k, ref in ((1, wk_ref), (2, wv_ref), (0, wq_ref))
        for side in range(sides)
    ]
    out_loads = [
        pltpu.make_async_copy(w_out_ref.at[:, pl.ds(j * chunk, chunk)], w_out.at[j], wo_sem.at[j]) for j in range(chunks)
    ]
    small_loads = [
        pltpu.make_async_copy(source, target, small_sem.at[k])
        for k, (source, target) in enumerate(((decay_in, decay_ref), (gain_in, gain_ref), (mask_in, mask_ref)))
    ]
    for load in loads + small_loads:
        load.start()

    barrier = pltpu.get_barrier_semaphore()
    for ahead in range(1, spans):
        pl.semaphore_signal(barrier, inc=1, device_id={"ctx": lax.rem(me + ahead, spans)}, device_id_type=MESH)
    for mask in partners:
        pl.semaphore_signal(barrier, inc=1, device_id={"head": flipped(lane, mask)}, device_id_type=MESH)
    pl.semaphore_wait(barrier, spans - 1 + len(partners))

    def exchange(span, source):
        return pltpu.make_async_remote_copy(
            src_ref=columns(span), dst_ref=xs.at[source, lane],
            send_sem=z_send.at[span], recv_sem=z_recv.at[source],
            device_id={"ctx": span}, device_id_type=MESH,
        )

    def send_rows(outward):
        for distance in range(1, spans):
            for target in (me + distance, me - distance):
                within = (target >= 0) & (target < spans)
                early = edge | ((target > me) == (2 * me > last))

                @pl.when(within & (early if outward else jnp.logical_not(early)))
                def _():
                    exchange(target, me).start()

    def send_aux(side):
        return pltpu.make_async_remote_copy(
            src_ref=aux_own.at[side], dst_ref=aux_all.at[me],
            send_sem=a_send.at[side], recv_sem=a_recv.at[me],
            device_id={"ctx": side * last}, device_id_type=MESH,
        )

    def take_aux(span):
        pltpu.make_async_remote_copy(
            src_ref=aux_own.at[0], dst_ref=aux_all.at[span],
            send_sem=a_send.at[0], recv_sem=a_recv.at[span],
            device_id={"ctx": lax.rem(me + 1, spans)}, device_id_type=MESH,
        ).wait_recv()

    def spread(span, mask):
        block = xs.at[span, lane]
        return pltpu.make_async_remote_copy(
            src_ref=block, dst_ref=block, send_sem=g_send.at[span, mask], recv_sem=g_recv.at[span, mask],
            device_id={"head": flipped(lane, mask)}, device_id_type=MESH,
        )

    def hand_across(span, mask):
        block = xs.at[span, flipped(lane, mask)]
        return pltpu.make_async_remote_copy(
            src_ref=block, dst_ref=block,
            send_sem=g_send.at[span, mask | bits[0]], recv_sem=g_recv.at[span, mask | bits[0]],
            device_id={"head": flipped(lane, bits[0])}, device_id_type=MESH,
        )

    def settled(span, mask):
        block = xs.at[span, flipped(lane, mask)]
        return pltpu.make_async_remote_copy(
            src_ref=block, dst_ref=block, send_sem=g_send.at[span, mask], recv_sem=g_recv.at[span, mask],
            device_id={"head": flipped(lane, bits[0])}, device_id_type=MESH,
        )

    per_place = 2 * chips
    needed, visits = [], []
    for device in range(spans):
        down = [LAG * (last - device) + per_place * (last - span) for span in range(spans)]
        up = [LAG * device + per_place * span for span in range(spans)]
        when = [min(pair_) for pair_ in zip(down, up)] if sides == 2 else down
        visits.append(sorted(range(spans), key=lambda span: when[span]))
        needed.append(sorted(when))
    needed = [min(device[k] for device in needed) for k in range(spans)]

    def visit(k):
        span = visits[0][k] + 0 * me
        for device in range(1, spans):
            span = jnp.where(me == device, visits[device][k], span)
        return span

    def begin(k):
        span = visit(k)

        @pl.when(me == span)
        def _():
            own.wait()

        @pl.when(me != span)
        def _():
            exchange(span, span).wait_recv()

        for mask in across_chips[1:]:
            spread(span, mask).start()

    def cross(k):
        span = visit(k)
        for mask in across_chips:
            if mask:
                settled(span, mask).wait_recv()
            hand_across(span, mask).start()

    def finish(k):
        span = visit(k)
        for mask in across_chips:
            settled(span, mask | bits[0]).wait_recv()

    def column(span, head):
        return span * aux_all.shape[1] + head

    def prepare():
        aux_all[me] = aux_own[my_side]
        for span in range(spans):

            @pl.when(me != span)
            def _():
                take_aux(span)

        logs = aux_all[...].reshape(spans * aux_all.shape[1], tokens)
        first = lax.broadcasted_iota(jnp.int32, (tokens, tokens), 0)
        second = lax.broadcasted_iota(jnp.int32, (tokens, tokens), 1)
        exact = lax.Precision.HIGHEST
        cum[...] = jnp.dot(
            logs, (first <= second).astype(jnp.float32), precision=exact, preferred_element_type=jnp.float32
        )
        cum_t[...] = lax.dot_general(
            (second <= first).astype(jnp.float32), logs, (((1,), (1,)), ((), ())),
            precision=exact, preferred_element_type=jnp.float32,
        )
        for span in range(spans):
            for head in range(own_heads):
                j = column(span, head)
                down, across = cum_t[:, j : j + 1], cum[j : j + 1, :]
                fade[span, head] = jnp.broadcast_to(jnp.exp(across[:, tokens - 1 :] - down), (tokens, HEAD_DIM))
                reach[span, head] = jnp.broadcast_to(jnp.exp(down), (tokens, HEAD_DIM))
                for a in range(per_span):
                    for e in range(per_span):
                        at = slice(a * BLOCK, (a + 1) * BLOCK), slice(e * BLOCK, (e + 1) * BLOCK)
                        if e > a:
                            shape[span, head, at[0], at[1]] = jnp.zeros((BLOCK, BLOCK), jnp.float32)
                            continue
                        level = (a ^ e).bit_length()
                        spread = down[at[0], :] - across[:, at[1]]
                        if e == a:
                            causal = lax.broadcasted_iota(jnp.int32, (BLOCK, BLOCK), 0) >= lax.broadcasted_iota(
                                jnp.int32, (BLOCK, BLOCK), 1
                            )
                            decay = jnp.where(causal, jnp.exp(jnp.where(causal, spread, 0.0)), 0.0)
                        else:
                            decay = jnp.exp(spread)
                        shape[span, head, at[0], at[1]] = decay * level_weight(span, a, head, level)

    def level_weight(span, a, head, level):
        held = aux_all[span, own_heads + a : own_heads + a + 1, level : level + 1]
        gain = gain_ref[head : head + 1, level : level + 1]
        if sides == 2:
            other = gain_ref[own_heads + head : own_heads + head + 1, level : level + 1]
            gain = jnp.where(my_side == 0, gain, other)
        return held * gain

    def absorb(place):
        span = jnp.where(my_side == 0, last - place, place)
        for head in range(own_heads):
            key = unit(part[my_side, 1, span, :, :, lanes(head)].reshape(tokens, HEAD_DIM))
            keys[span, head] = key
            decayed = (key.astype(jnp.float32) * fade[span, head]).astype(jnp.bfloat16)
            value = part[my_side, 2, span, :, :, lanes(head)].reshape(tokens, HEAD_DIM)
            state[span, head] = lax.dot_general(
                decayed, value, (((0,), (0,)), ((), ())), preferred_element_type=jnp.float32
            )

    def combine():
        for head in range(own_heads):
            totals = [cum[column(s, head) : column(s, head) + 1, tokens - 1 :] for s in range(spans)]
            for span in range(spans):
                carried = {}
                between = jnp.zeros_like(totals[0])
                for e in range(span - 1, -1, -1):
                    m = (span ^ e).bit_length() - 1
                    term = state[e, head] * jnp.exp(between)
                    carried[m] = carried[m] + term if m in carried else term
                    between = between + totals[e]
                for a in range(per_span):
                    mixed = jnp.zeros((HEAD_DIM, HEAD_DIM), jnp.float32)
                    for m, held in carried.items():
                        mixed = mixed + held * level_weight(span, a, head, (2**m * per_span).bit_length())
                    effect[span, a, head] = mixed.astype(jnp.bfloat16)

    def hand_over(span, d):
        return pltpu.make_async_remote_copy(
            src_ref=ho_out.at[span, d], dst_ref=ho.at[my_side, d],
            send_sem=h_send.at[span, d], recv_sem=h_recv.at[my_side, d],
            device_id={"ctx": span}, device_id_type=MESH,
        )

    def handed(j):
        for span in range(spans):

            @pl.when(owner & (me != span))
            def _():
                hand_over(span, exclusive(chip, j, chips)).wait_send()

    def take_heads(side, d):
        pltpu.make_async_remote_copy(
            src_ref=ho_out.at[0, d], dst_ref=ho.at[side, d],
            send_sem=h_send.at[0, d], recv_sem=h_recv.at[side, d],
            device_id={"ctx": lax.rem(me + 1, spans)}, device_id_type=MESH,
        ).wait_recv()

    def respond(span, d):
        inside = pl.ds(pl.multiple_of(d * tile_rows, tile_rows), tile_rows)
        query = [unit(part[my_side, 0, span, d, :, lanes(head)]) for head in range(own_heads)]
        scores = [
            lax.dot_general(
                query[head], keys[span, head], (((1,), (1,)), ((), ())), preferred_element_type=jnp.float32
            )
            for head in range(own_heads)
        ]
        far = [
            jnp.dot(
                (query[head].astype(jnp.float32) * reach[span, head, inside, :]).astype(jnp.bfloat16),
                effect[span, d // per_block, head], preferred_element_type=jnp.float32,
            )
            for head in range(own_heads)
        ]
        shaped = [(scores[head] * shape[span, head, inside, :]).astype(jnp.bfloat16) for head in range(own_heads)]
        for head in range(own_heads):
            value = part[my_side, 2, span, :, :, lanes(head)].reshape(tokens, HEAD_DIM)
            near = jnp.dot(shaped[head], value, preferred_element_type=jnp.float32)
            ho_out[span, d, :, lanes(head)] = (near + far[head]).astype(jnp.bfloat16)

        @pl.when(span == me)
        def _():
            ho[my_side, d] = ho_out[span, d]

        @pl.when(span != me)
        def _():
            hand_over(span, d).start()

    def attend(i, span, d):
        @pl.when((i < kv_tiles) & (i % per_place == per_place - 1))
        def _():
            absorb(i // per_place)

        pl.when(i == kv_tiles - 1)(combine)

        @pl.when(i >= kv_tiles)
        def _():
            respond(span, d)

    def link(side, i, kind, span, d):
        step = jnp.where(side == 0, -1, 1)
        k = (kind * spans + span) * chips + d
        return pltpu.make_async_remote_copy(
            src_ref=part.at[side, kind, span, d], dst_ref=inbox.at[side, kind, span, d],
            send_sem=p_send.at[side, i], recv_sem=p_recv.at[side, k],
            device_id={"ctx": lax.rem(me + step + spans, spans)}, device_id_type=MESH,
        )

    def place_in_chain(side):
        return jnp.where(side == 0, last - me, me)

    def add_tile(side, t, may_own):
        p = place_in_chain(side)
        i = t - LAG * p

        @pl.when((i >= 0) & (i < tiles))
        def _():
            late = i >= kv_tiles
            pos = jnp.where(late, (i - kv_tiles) % spans, i // per_place)
            kind = jnp.where(late, 0, 1 + (i % per_place) // chips)
            span = jnp.where(side == 0, last - pos, pos)
            d = exclusive(chip, jnp.where(late, chips - 1 - (i - kv_tiles) // spans, i % chips), chips)
            block = xs[span, pl.ds(2 * d, 2)]
            if rows % 16:
                block = block.astype(jnp.float32)
            block = block.reshape(tile_rows, depth).astype(jnp.bfloat16)
            product = jnp.dot(block, weight[side, kind], preferred_element_type=jnp.float32)

            @pl.when(p == 0)
            def _():
                part[side, kind, span, d] = product.astype(jnp.bfloat16)

            @pl.when(p > 0)
            def _():
                link(side, i, kind, span, d).wait_recv()
                added = product + inbox[side, kind, span, d].astype(jnp.float32)
                part[side, kind, span, d] = added.astype(jnp.bfloat16)

            @pl.when(p < last)
            def _():
                link(side, i, kind, span, d).start()

            if may_own:

                @pl.when(p == last)
                def _():
                    attend(i, span, d)

        @pl.when((p < last) & (i >= KEPT) & (i < tiles + KEPT))
        def _():
            link(side, i - KEPT, 0, 0, 0).wait_send()

    def to_sibling(j):
        return pltpu.make_async_remote_copy(
            src_ref=share.at[j, 1 - core], dst_ref=beside.at[j],
            send_sem=b_send.at[j], recv_sem=b_recv.at[j],
            device_id={"head": flipped(lane, 1)}, device_id_type=MESH,
        )

    def to_owner(j):
        return pltpu.make_async_remote_copy(
            src_ref=share.at[j, core], dst_ref=arrived.at[j],
            send_sem=s_send.at[j], recv_sem=s_recv.at[j],
            device_id={"head": 2 * exclusive(chip, j, chips) + core}, device_id_type=MESH,
        )

    def emit(j):
        d = exclusive(chip, j, chips)
        for side in range(sides):

            @pl.when(me != side * last)
            def _():
                take_heads(side, d)

        for c in range(chunks):
            product = None
            for side in range(sides):
                term = jnp.dot(
                    ho[side, d], w_out[c, side * width : (side + 1) * width, :], preferred_element_type=jnp.float32
                )
                product = term if product is None else product + term
            for k in range(2):
                share[j, k, :, c * chunk : (c + 1) * chunk] = product[k * rows : (k + 1) * rows, :].astype(jnp.bfloat16)
        to_sibling(j).start()

    def settle(j):
        to_sibling(j).wait_recv()
        for c in range(chunks):
            at = slice(c * chunk, (c + 1) * chunk)
            added = share[j, core, :, at].astype(jnp.float32) + beside[j, :, at].astype(jnp.float32)
            share[j, core, :, at] = added.astype(jnp.bfloat16)

        @pl.when(j > 0)
        def _():
            to_owner(j).start()

        @pl.when(j < chips - 1)
        def _():
            handed(j + 1)

    first_out = kv_tiles + LAG * last + last + AFTER
    end = first_out + spans * (chips - 1) + PAUSE + 1

    def give(t):
        for offset, act in ((0, emit), (PAUSE, settle)):
            after = t - first_out - offset

            @pl.when((after >= 0) & (after % spans == 0) & (after < spans * chips))
            def _():
                act(chips - 1 - after // spans)

    if sides == 2:
        first_side = jnp.where(me < last - me, 1, 0)
        order = [first_side, 1 - first_side]
    else:
        order = [0]

    def steps(start, stop):
        def body(t, carry):
            for which, side in enumerate(order):
                add_tile(side, t, which == sides - 1 and stop > LAG * last)
            if stop > first_out:
                give(t)
            return carry

        lax.fori_loop(start, stop, body, 0)

    send_rows(True)
    events = {}
    for k in range(spans):
        at = max(needed[k] - 2, 0) if k else -1
        events.setdefault(at, []).append((1, k))
        events.setdefault(max(needed[k], 0) if k else -1, []).append((2, k))
        events.setdefault(-1 if k < 3 else max(needed[k - 2] - 2, 0), []).append((0, k))
    for load in small_loads:
        load.wait()
    begin(0)
    if spans > 1:
        begin(1)
    send_rows(False)
    cross(0)
    if spans > 2:
        begin(2)
    aux_own[...] = jnp.zeros_like(aux_own)
    for side in range(sides):
        aux_own[side, :own_heads, :] = decay_ref[side * own_heads : (side + 1) * own_heads, :]
        aux_own[side, own_heads : own_heads + per_span, : mask_ref.shape[1]] = mask_ref[...].astype(jnp.float32)
    for side in range(sides):

        @pl.when(me != side * last)
        def _():
            send_aux(side).start()

    for load in loads:
        load.wait()
    for load in out_loads:
        load.start()
    finish(0)
    done, act = 0, (begin, cross, finish, lambda _: pl.when(owner)(prepare))
    events.setdefault(LAG * last, []).append((3, 0))
    for at in sorted(key for key in events if key >= 0):
        if at > done:
            steps(done, at)
            done = at
        for action, k in sorted(events[at], key=lambda event: -event[0] % 4):
            act[action](k)
    steps(done, LAG * last + per_place)
    for distance in range(1, spans):
        exchange(lax.rem(me + distance, spans), me).wait_send()
    for span in range(spans):
        for mask in range(1, heads):
            settled(span, mask).wait_send()
    for side in range(sides):

        @pl.when(me != side * last)
        def _():
            send_aux(side).wait_send()
    for load in out_loads:
        load.wait()
    steps(LAG * last + per_place, end)
    for c in range(chunks):
        at = slice(c * chunk, (c + 1) * chunk)
        added = share[0, core, :, at].astype(jnp.float32)
        for j in range(chips - 1, 0, -1):
            if c == 0:
                to_owner(j).wait_recv()
            added = added + arrived[j, :, at].astype(jnp.float32)
        out_ref[:, at] = added.astype(jnp.bfloat16)

    for j in range(chips):
        to_sibling(j).wait_send()
        if j:
            to_owner(j).wait_send()
    handed(0)


def on_device(layer_input, w_query, w_key, w_value, w_out, log_decay, level_gain, level_mask):
    spans, heads = lax.axis_size("ctx"), lax.axis_size("head")
    rows, model = layer_input.shape
    depth, columns = w_query.shape
    local_heads, tokens = log_decay.shape
    sides = 2 if local_heads % 2 == 0 and spans > 1 else 1
    width = columns // sides
    own_heads = local_heads // sides
    per_span = tokens // BLOCK
    chips, tile_rows = heads // 2, 2 * rows
    tiles = 3 * chips * spans
    aux_rows = -(-(own_heads + per_span) // 8) * 8
    chunk = model // CHUNKS
    dma = pltpu.SemaphoreType.DMA
    hbm = pl.BlockSpec(memory_space=pl.ANY)
    vmem = pl.BlockSpec(memory_space=pltpu.VMEM)
    half, full = jnp.bfloat16, jnp.float32
    return pl.pallas_call(
        functools.partial(layer_kernel, spans, heads),
        out_shape=jax.ShapeDtypeStruct((rows, model), half),
        in_specs=[hbm] * 8,
        out_specs=vmem,
        scratch_shapes=[
            pltpu.VMEM(log_decay.shape, log_decay.dtype),
            pltpu.VMEM(level_gain.shape, level_gain.dtype),
            pltpu.VMEM(level_mask.shape, level_mask.dtype),
            pltpu.VMEM((spans, heads, rows, depth), half),
            pltpu.VMEM((sides, 3, depth, width), half),
            pltpu.VMEM((sides, 3, spans, chips, tile_rows, width), half),
            pltpu.VMEM((sides, 3, spans, chips, tile_rows, width), half),
            pltpu.VMEM((sides, aux_rows, tokens), full),
            pltpu.VMEM((spans, aux_rows, tokens), full),
            pltpu.VMEM((spans * aux_rows, tokens), full),
            pltpu.VMEM((tokens, spans * aux_rows), full),
            pltpu.VMEM((spans, own_heads, tokens, tokens), full),
            pltpu.VMEM((spans, own_heads, tokens, HEAD_DIM), full),
            pltpu.VMEM((spans, own_heads, tokens, HEAD_DIM), full),
            pltpu.VMEM((spans, own_heads, tokens, HEAD_DIM), half),
            pltpu.VMEM((spans, own_heads, HEAD_DIM, HEAD_DIM), full),
            pltpu.VMEM((spans, per_span, own_heads, HEAD_DIM, HEAD_DIM), half),
            pltpu.VMEM((spans, chips, tile_rows, width), half),
            pltpu.VMEM((sides, chips, tile_rows, width), half),
            pltpu.VMEM((CHUNKS, columns, chunk), half),
            pltpu.VMEM((chips, 2, rows, model), half),
            pltpu.VMEM((chips, rows, model), half),
            pltpu.VMEM((chips, rows, model), half),
            dma((3,)), dma((sides, 3)), dma((CHUNKS,)), dma((spans,)), dma((spans,)), dma,
            dma((spans, heads)), dma((spans, heads)),
            dma((sides, tiles)), dma((sides, tiles)),
            dma((sides,)), dma((spans,)),
            dma((spans, chips)), dma((sides, chips)),
            dma((chips,)), dma((chips,)), dma((chips,)), dma((chips,)),
        ],
        compiler_params=pltpu.CompilerParams(collective_id=0, has_side_effects=True, vmem_limit_bytes=VMEM_LIMIT),
        name="layer",
    )(layer_input, w_query, w_key, w_value, w_out, log_decay, level_gain, level_mask)


def solution(mesh):
    in_specs = (
        P(("ctx", "head"), None),
        P("ctx", "head"),
        P("ctx", "head"),
        P("ctx", "head"),
        P("head", None),
        P("head", "ctx"),
        P("head", None),
        P("ctx", None),
    )
    out_specs = P(("ctx", "head"), None)
    return jax.shard_map(
        on_device, mesh=mesh, in_specs=in_specs, out_specs=out_specs, check_vma=False
    )
```

```python
import functools

import jax
import jax.numpy as jnp
from jax import lax
from jax.experimental import pallas as pl
from jax.experimental.pallas import tpu as pltpu
from jax.sharding import PartitionSpec as P

HEAD_DIM = 128
BLOCK = 128
LAG = 5
AFTER = 3
PAUSE = 2
KEPT = 5
CUTS = 2
CHUNKS = 4
VMEM_LIMIT = 60 * 2**20
MESH = pl.DeviceIdType.MESH


def flipped(index, mask):
    bit = 1
    while bit <= mask:
        if mask & bit:
            index = index + bit - 2 * bit * ((index // bit) % 2)
        bit *= 2
    return index


def subsets(bits):
    masks = [0]
    for bit in bits:
        masks = masks + [mask | bit for mask in masks]
    return masks


def bits_of(count):
    return [2**k for k in range(count.bit_length() - 1)]


def exclusive(first, second, count):
    result = 0
    for bit in bits_of(count):
        x, y = (first // bit) % 2, (second // bit) % 2
        result = result + (x + y - 2 * x * y) * bit
    return result


def unit(block):
    floated = block.astype(jnp.float32)
    return (floated * lax.rsqrt(jnp.sum(floated * floated, axis=-1, keepdims=True) + 1e-06)).astype(jnp.bfloat16)


def lanes(head):
    return slice(head * HEAD_DIM, (head + 1) * HEAD_DIM)


def layer_kernel(
    spans, heads, x_ref, wq_ref, wk_ref, wv_ref, w_out_ref, decay_in, gain_in, mask_in, arrived,
    decay_ref, gain_ref, mask_ref,
    xs, weight, part, inbox, aux_own, aux_all, cum, cum_t, shape, fade, reach, keys, state, effect,
    ho_out, ho, w_out, share, beside,
    small_sem, w_sem, wo_sem, z_send, z_recv, own_sem, g_send, g_recv, p_send, p_recv, a_send, a_recv, h_send, h_recv, b_send, b_recv, s_send, s_recv, last_sem,
):
    me, lane = lax.axis_index("ctx"), lax.axis_index("head")
    rows = x_ref.shape[0]
    sides, _, depth, width = weight.shape
    own_heads = width // HEAD_DIM
    tokens = heads * rows
    per_span = tokens // BLOCK
    chips = heads // 2
    chip, core = lane // 2, lane % 2
    tile_rows = 2 * rows
    per_block = BLOCK // tile_rows
    tiles, kv_tiles = 3 * chips * spans, 2 * chips * spans
    chunks, chunk = CHUNKS, w_out.shape[-1]
    bits = bits_of(heads)
    across_chips = subsets(bits[1:])
    partners = across_chips[1:] + bits[:1]
    last = spans - 1
    edge = (me == 0) | (me == last)
    my_side = jnp.where(me == 0, 0, sides - 1)
    owner = edge if sides == 2 else me == 0

    def columns(span):
        return x_ref.at[:, pl.ds(pl.multiple_of(span * depth, depth), depth)]

    own = pltpu.make_async_copy(columns(me), xs.at[me, lane], own_sem)
    own.start()
    loads = [
        pltpu.make_async_copy(ref.at[:, pl.ds(side * width, width)], weight.at[side, k], w_sem.at[side, k])
        for k, ref in ((1, wk_ref), (2, wv_ref), (0, wq_ref))
        for side in range(sides)
    ]
    out_loads = [
        pltpu.make_async_copy(w_out_ref.at[:, pl.ds(j * chunk, chunk)], w_out.at[j], wo_sem.at[j]) for j in range(chunks)
    ]
    small_loads = [
        pltpu.make_async_copy(source, target, small_sem.at[k])
        for k, (source, target) in enumerate(((decay_in, decay_ref), (gain_in, gain_ref), (mask_in, mask_ref)))
    ]
    for load in loads + small_loads:
        load.start()

    barrier = pltpu.get_barrier_semaphore()
    for ahead in range(1, spans):
        pl.semaphore_signal(barrier, inc=1, device_id={"ctx": lax.rem(me + ahead, spans)}, device_id_type=MESH)
    for mask in partners:
        pl.semaphore_signal(barrier, inc=1, device_id={"head": flipped(lane, mask)}, device_id_type=MESH)
    pl.semaphore_wait(barrier, spans - 1 + len(partners))

    def exchange(span, source):
        return pltpu.make_async_remote_copy(
            src_ref=columns(span), dst_ref=xs.at[source, lane],
            send_sem=z_send.at[span], recv_sem=z_recv.at[source],
            device_id={"ctx": span}, device_id_type=MESH,
        )

    def send_rows(outward):
        for distance in range(1, spans):
            for target in (me + distance, me - distance):
                within = (target >= 0) & (target < spans)
                early = edge | ((target > me) == (2 * me > last))

                @pl.when(within & (early if outward else jnp.logical_not(early)))
                def _():
                    exchange(target, me).start()

    def send_aux(side):
        return pltpu.make_async_remote_copy(
            src_ref=aux_own.at[side], dst_ref=aux_all.at[me],
            send_sem=a_send.at[side], recv_sem=a_recv.at[me],
            device_id={"ctx": side * last}, device_id_type=MESH,
        )

    def take_aux(span):
        pltpu.make_async_remote_copy(
            src_ref=aux_own.at[0], dst_ref=aux_all.at[span],
            send_sem=a_send.at[0], recv_sem=a_recv.at[span],
            device_id={"ctx": lax.rem(me + 1, spans)}, device_id_type=MESH,
        ).wait_recv()

    def spread(span, mask):
        block = xs.at[span, lane]
        return pltpu.make_async_remote_copy(
            src_ref=block, dst_ref=block, send_sem=g_send.at[span, mask], recv_sem=g_recv.at[span, mask],
            device_id={"head": flipped(lane, mask)}, device_id_type=MESH,
        )

    def hand_across(span, mask):
        block = xs.at[span, flipped(lane, mask)]
        return pltpu.make_async_remote_copy(
            src_ref=block, dst_ref=block,
            send_sem=g_send.at[span, mask | bits[0]], recv_sem=g_recv.at[span, mask | bits[0]],
            device_id={"head": flipped(lane, bits[0])}, device_id_type=MESH,
        )

    def settled(span, mask):
        block = xs.at[span, flipped(lane, mask)]
        return pltpu.make_async_remote_copy(
            src_ref=block, dst_ref=block, send_sem=g_send.at[span, mask], recv_sem=g_recv.at[span, mask],
            device_id={"head": flipped(lane, bits[0])}, device_id_type=MESH,
        )

    per_place = 2 * chips
    needed, visits = [], []
    for device in range(spans):
        down = [LAG * (last - device) + per_place * (last - span) for span in range(spans)]
        up = [LAG * device + per_place * span for span in range(spans)]
        when = [min(pair_) for pair_ in zip(down, up)] if sides == 2 else down
        visits.append(sorted(range(spans), key=lambda span: when[span]))
        needed.append(sorted(when))
    needed = [min(device[k] for device in needed) for k in range(spans)]

    def visit(k):
        span = visits[0][k] + 0 * me
        for device in range(1, spans):
            span = jnp.where(me == device, visits[device][k], span)
        return span

    def begin(k):
        span = visit(k)

        @pl.when(me == span)
        def _():
            own.wait()

        @pl.when(me != span)
        def _():
            exchange(span, span).wait_recv()

        for mask in across_chips[1:]:
            spread(span, mask).start()

    def cross(k):
        span = visit(k)
        for mask in across_chips:
            if mask:
                settled(span, mask).wait_recv()
            hand_across(span, mask).start()

    def finish(k):
        span = visit(k)
        for mask in across_chips:
            settled(span, mask | bits[0]).wait_recv()

    def column(span, head):
        return span * aux_all.shape[1] + head

    def prepare():
        aux_all[me] = aux_own[my_side]
        for span in range(spans):

            @pl.when(me != span)
            def _():
                take_aux(span)

        logs = aux_all[...].reshape(spans * aux_all.shape[1], tokens)
        first = lax.broadcasted_iota(jnp.int32, (tokens, tokens), 0)
        second = lax.broadcasted_iota(jnp.int32, (tokens, tokens), 1)
        exact = lax.Precision.HIGHEST
        cum[...] = jnp.dot(
            logs, (first <= second).astype(jnp.float32), precision=exact, preferred_element_type=jnp.float32
        )
        cum_t[...] = lax.dot_general(
            (second <= first).astype(jnp.float32), logs, (((1,), (1,)), ((), ())),
            precision=exact, preferred_element_type=jnp.float32,
        )
        for span in range(spans):
            for head in range(own_heads):
                j = column(span, head)
                down, across = cum_t[:, j : j + 1], cum[j : j + 1, :]
                fade[span, head] = jnp.broadcast_to(jnp.exp(across[:, tokens - 1 :] - down), (tokens, HEAD_DIM))
                reach[span, head] = jnp.broadcast_to(jnp.exp(down), (tokens, HEAD_DIM))
                for a in range(per_span):
                    for e in range(per_span):
                        at = slice(a * BLOCK, (a + 1) * BLOCK), slice(e * BLOCK, (e + 1) * BLOCK)
                        if e > a:
                            shape[span, head, at[0], at[1]] = jnp.zeros((BLOCK, BLOCK), jnp.float32)
                            continue
                        level = (a ^ e).bit_length()
                        spread = down[at[0], :] - across[:, at[1]]
                        if e == a:
                            causal = lax.broadcasted_iota(jnp.int32, (BLOCK, BLOCK), 0) >= lax.broadcasted_iota(
                                jnp.int32, (BLOCK, BLOCK), 1
                            )
                            decay = jnp.where(causal, jnp.exp(jnp.where(causal, spread, 0.0)), 0.0)
                        else:
                            decay = jnp.exp(spread)
                        shape[span, head, at[0], at[1]] = decay * level_weight(span, a, head, level)

    def level_weight(span, a, head, level):
        held = aux_all[span, own_heads + a : own_heads + a + 1, level : level + 1]
        gain = gain_ref[head : head + 1, level : level + 1]
        if sides == 2:
            other = gain_ref[own_heads + head : own_heads + head + 1, level : level + 1]
            gain = jnp.where(my_side == 0, gain, other)
        return held * gain

    def absorb(place):
        span = jnp.where(my_side == 0, last - place, place)
        for head in range(own_heads):
            key = unit(part[my_side, 1, span, :, :, lanes(head)].reshape(tokens, HEAD_DIM))
            keys[span, head] = key
            decayed = (key.astype(jnp.float32) * fade[span, head]).astype(jnp.bfloat16)
            value = part[my_side, 2, span, :, :, lanes(head)].reshape(tokens, HEAD_DIM)
            state[span, head] = lax.dot_general(
                decayed, value, (((0,), (0,)), ((), ())), preferred_element_type=jnp.float32
            )

    def combine():
        for head in range(own_heads):
            totals = [cum[column(s, head) : column(s, head) + 1, tokens - 1 :] for s in range(spans)]
            for span in range(spans):
                carried = {}
                between = jnp.zeros_like(totals[0])
                for e in range(span - 1, -1, -1):
                    m = (span ^ e).bit_length() - 1
                    term = state[e, head] * jnp.exp(between)
                    carried[m] = carried[m] + term if m in carried else term
                    between = between + totals[e]
                for a in range(per_span):
                    mixed = jnp.zeros((HEAD_DIM, HEAD_DIM), jnp.float32)
                    for m, held in carried.items():
                        mixed = mixed + held * level_weight(span, a, head, (2**m * per_span).bit_length())
                    effect[span, a, head] = mixed.astype(jnp.bfloat16)

    def hand_over(span, d):
        return pltpu.make_async_remote_copy(
            src_ref=ho_out.at[span, d], dst_ref=ho.at[my_side, d],
            send_sem=h_send.at[span, d], recv_sem=h_recv.at[my_side, d],
            device_id={"ctx": span}, device_id_type=MESH,
        )

    def handed(j):
        for span in range(spans):

            @pl.when(owner & (me != span))
            def _():
                hand_over(span, exclusive(chip, j, chips)).wait_send()

    def take_heads(side, d):
        pltpu.make_async_remote_copy(
            src_ref=ho_out.at[0, d], dst_ref=ho.at[side, d],
            send_sem=h_send.at[0, d], recv_sem=h_recv.at[side, d],
            device_id={"ctx": lax.rem(me + 1, spans)}, device_id_type=MESH,
        ).wait_recv()

    def respond(span, d):
        inside = pl.ds(pl.multiple_of(d * tile_rows, tile_rows), tile_rows)
        query = [unit(part[my_side, 0, span, d, :, lanes(head)]) for head in range(own_heads)]
        scores = [
            lax.dot_general(
                query[head], keys[span, head], (((1,), (1,)), ((), ())), preferred_element_type=jnp.float32
            )
            for head in range(own_heads)
        ]
        far = [
            jnp.dot(
                (query[head].astype(jnp.float32) * reach[span, head, inside, :]).astype(jnp.bfloat16),
                effect[span, d // per_block, head], preferred_element_type=jnp.float32,
            )
            for head in range(own_heads)
        ]
        shaped = [(scores[head] * shape[span, head, inside, :]).astype(jnp.bfloat16) for head in range(own_heads)]
        for head in range(own_heads):
            value = part[my_side, 2, span, :, :, lanes(head)].reshape(tokens, HEAD_DIM)
            near = jnp.dot(shaped[head], value, preferred_element_type=jnp.float32)
            ho_out[span, d, :, lanes(head)] = (near + far[head]).astype(jnp.bfloat16)

        @pl.when(span == me)
        def _():
            ho[my_side, d] = ho_out[span, d]

        @pl.when(span != me)
        def _():
            hand_over(span, d).start()

    def attend(i, span, d):
        @pl.when((i < kv_tiles) & (i % per_place == per_place - 1))
        def _():
            absorb(i // per_place)

        pl.when(i == kv_tiles - 1)(combine)

        @pl.when(i >= kv_tiles)
        def _():
            respond(span, d)

    def link(side, i, kind, span, d):
        step = jnp.where(side == 0, -1, 1)
        k = (kind * spans + span) * chips + d
        return pltpu.make_async_remote_copy(
            src_ref=part.at[side, kind, span, d], dst_ref=inbox.at[side, kind, span, d],
            send_sem=p_send.at[side, i], recv_sem=p_recv.at[side, k],
            device_id={"ctx": lax.rem(me + step + spans, spans)}, device_id_type=MESH,
        )

    def place_in_chain(side):
        return jnp.where(side == 0, last - me, me)

    def add_tile(side, t, may_own):
        p = place_in_chain(side)
        i = t - LAG * p

        @pl.when((i >= 0) & (i < tiles))
        def _():
            late = i >= kv_tiles
            pos = jnp.where(late, (i - kv_tiles) % spans, i // per_place)
            kind = jnp.where(late, 0, 1 + (i % per_place) // chips)
            span = jnp.where(side == 0, last - pos, pos)
            d = exclusive(chip, jnp.where(late, chips - 1 - (i - kv_tiles) // spans, i % chips), chips)
            block = xs[span, pl.ds(2 * d, 2)]
            if rows % 16:
                block = block.astype(jnp.float32)
            block = block.reshape(tile_rows, depth).astype(jnp.bfloat16)
            product = jnp.dot(block, weight[side, kind], preferred_element_type=jnp.float32)

            @pl.when(p == 0)
            def _():
                part[side, kind, span, d] = product.astype(jnp.bfloat16)

            @pl.when(p > 0)
            def _():
                link(side, i, kind, span, d).wait_recv()
                added = product + inbox[side, kind, span, d].astype(jnp.float32)
                part[side, kind, span, d] = added.astype(jnp.bfloat16)

            @pl.when(p < last)
            def _():
                link(side, i, kind, span, d).start()

            if may_own:

                @pl.when(p == last)
                def _():
                    attend(i, span, d)

        @pl.when((p < last) & (i >= KEPT) & (i < tiles + KEPT))
        def _():
            link(side, i - KEPT, 0, 0, 0).wait_send()

    cut = chunks * chunk // CUTS

    def to_sibling(j, q):
        at = pl.ds(q * cut, cut)
        return pltpu.make_async_remote_copy(
            src_ref=share.at[j, 1 - core, :, at], dst_ref=beside.at[j, :, at],
            send_sem=b_send.at[j, q], recv_sem=b_recv.at[j, q],
            device_id={"head": flipped(lane, 1)}, device_id_type=MESH,
        )

    def to_owner(j, q):
        at = pl.ds(q * cut, cut)
        return pltpu.make_async_remote_copy(
            src_ref=share.at[j, core, :, at], dst_ref=arrived.at[j, :, at],
            send_sem=s_send.at[j, q], recv_sem=s_recv.at[j, q],
            device_id={"head": 2 * exclusive(chip, j, chips) + core}, device_id_type=MESH,
        )

    def emit(j):
        d = exclusive(chip, j, chips)
        for side in range(sides):

            @pl.when(me != side * last)
            def _():
                take_heads(side, d)

        for c in range(chunks):
            product = None
            for side in range(sides):
                term = jnp.dot(
                    ho[side, d], w_out[c, side * width : (side + 1) * width, :], preferred_element_type=jnp.float32
                )
                product = term if product is None else product + term
            for k in range(2):
                share[j, k, :, c * chunk : (c + 1) * chunk] = product[k * rows : (k + 1) * rows, :].astype(jnp.bfloat16)
            if (c + 1) % (chunks // CUTS) == 0:
                to_sibling(j, c // (chunks // CUTS)).start()

    def settle(j):
        for c in range(chunks):
            if c % (chunks // CUTS) == 0:
                to_sibling(j, c // (chunks // CUTS)).wait_recv()
            at = slice(c * chunk, (c + 1) * chunk)
            added = share[j, core, :, at].astype(jnp.float32) + beside[j, :, at].astype(jnp.float32)
            share[j, core, :, at] = added.astype(jnp.bfloat16)
            if (c + 1) % (chunks // CUTS) == 0:

                @pl.when(j > 0)
                def _():
                    to_owner(j, c // (chunks // CUTS)).start()

        @pl.when(j < chips - 1)
        def _():
            handed(j + 1)

    first_out = kv_tiles + LAG * last + last + AFTER
    end = first_out + spans * (chips - 1) + PAUSE + 1

    def give(t):
        for offset, act in ((0, emit), (PAUSE, settle)):
            after = t - first_out - offset

            @pl.when((after >= 0) & (after % spans == 0) & (after < spans * chips))
            def _():
                act(chips - 1 - after // spans)

    if sides == 2:
        first_side = jnp.where(me < last - me, 1, 0)
        order = [first_side, 1 - first_side]
    else:
        order = [0]

    def steps(start, stop):
        def body(t, carry):
            for which, side in enumerate(order):
                add_tile(side, t, which == sides - 1 and stop > LAG * last)
            if stop > first_out:
                give(t)
            return carry

        lax.fori_loop(start, stop, body, 0)

    send_rows(True)
    events = {}
    for k in range(spans):
        at = max(needed[k] - 2, 0) if k else -1
        events.setdefault(at, []).append((1, k))
        events.setdefault(max(needed[k], 0) if k else -1, []).append((2, k))
        events.setdefault(-1 if k < 3 else max(needed[k - 2] - 2, 0), []).append((0, k))
    for load in small_loads:
        load.wait()
    begin(0)
    if spans > 1:
        begin(1)
    send_rows(False)
    cross(0)
    if spans > 2:
        begin(2)
    aux_own[...] = jnp.zeros_like(aux_own)
    for side in range(sides):
        aux_own[side, :own_heads, :] = decay_ref[side * own_heads : (side + 1) * own_heads, :]
        aux_own[side, own_heads : own_heads + per_span, : mask_ref.shape[1]] = mask_ref[...].astype(jnp.float32)
    for side in range(sides):

        @pl.when(me != side * last)
        def _():
            send_aux(side).start()

    for load in loads:
        load.wait()
    for load in out_loads:
        load.start()
    finish(0)
    done, act = 0, (begin, cross, finish, lambda _: pl.when(owner)(prepare))
    events.setdefault(LAG * last, []).append((3, 0))
    for at in sorted(key for key in events if key >= 0):
        if at > done:
            steps(done, at)
            done = at
        for action, k in sorted(events[at], key=lambda event: -event[0] % 4):
            act[action](k)
    steps(done, LAG * last + per_place)
    for distance in range(1, spans):
        exchange(lax.rem(me + distance, spans), me).wait_send()
    for span in range(spans):
        for mask in range(1, heads):
            settled(span, mask).wait_send()
    for side in range(sides):

        @pl.when(me != side * last)
        def _():
            send_aux(side).wait_send()
    for load in out_loads:
        load.wait()
    steps(LAG * last + per_place, end)
    kept = pltpu.make_async_copy(share.at[0, core], arrived.at[0], last_sem)
    kept.start()
    for j in range(chips - 1, 0, -1):
        for q in range(CUTS):
            to_owner(j, q).wait_recv()

    for j in range(chips):
        for q in range(CUTS):
            to_sibling(j, q).wait_send()
            if j:
                to_owner(j, q).wait_send()
    handed(0)
    kept.wait()


def on_device(layer_input, w_query, w_key, w_value, w_out, log_decay, level_gain, level_mask):
    spans, heads = lax.axis_size("ctx"), lax.axis_size("head")
    rows, model = layer_input.shape
    depth, columns = w_query.shape
    local_heads, tokens = log_decay.shape
    sides = 2 if local_heads % 2 == 0 and spans > 1 else 1
    width = columns // sides
    own_heads = local_heads // sides
    per_span = tokens // BLOCK
    chips, tile_rows = heads // 2, 2 * rows
    tiles = 3 * chips * spans
    aux_rows = -(-(own_heads + per_span) // 8) * 8
    chunk = model // CHUNKS
    dma = pltpu.SemaphoreType.DMA
    hbm = pl.BlockSpec(memory_space=pl.ANY)
    half, full = jnp.bfloat16, jnp.float32
    shares = pl.pallas_call(
        functools.partial(layer_kernel, spans, heads),
        out_shape=jax.ShapeDtypeStruct((chips, rows, model), half),
        in_specs=[hbm] * 8,
        out_specs=hbm,
        scratch_shapes=[
            pltpu.VMEM(log_decay.shape, log_decay.dtype),
            pltpu.VMEM(level_gain.shape, level_gain.dtype),
            pltpu.VMEM(level_mask.shape, level_mask.dtype),
            pltpu.VMEM((spans, heads, rows, depth), half),
            pltpu.VMEM((sides, 3, depth, width), half),
            pltpu.VMEM((sides, 3, spans, chips, tile_rows, width), half),
            pltpu.VMEM((sides, 3, spans, chips, tile_rows, width), half),
            pltpu.VMEM((sides, aux_rows, tokens), full),
            pltpu.VMEM((spans, aux_rows, tokens), full),
            pltpu.VMEM((spans * aux_rows, tokens), full),
            pltpu.VMEM((tokens, spans * aux_rows), full),
            pltpu.VMEM((spans, own_heads, tokens, tokens), full),
            pltpu.VMEM((spans, own_heads, tokens, HEAD_DIM), full),
            pltpu.VMEM((spans, own_heads, tokens, HEAD_DIM), full),
            pltpu.VMEM((spans, own_heads, tokens, HEAD_DIM), half),
            pltpu.VMEM((spans, own_heads, HEAD_DIM, HEAD_DIM), full),
            pltpu.VMEM((spans, per_span, own_heads, HEAD_DIM, HEAD_DIM), half),
            pltpu.VMEM((spans, chips, tile_rows, width), half),
            pltpu.VMEM((sides, chips, tile_rows, width), half),
            pltpu.VMEM((CHUNKS, columns, chunk), half),
            pltpu.VMEM((chips, 2, rows, model), half),
            pltpu.VMEM((chips, rows, model), half),
            dma((3,)), dma((sides, 3)), dma((CHUNKS,)), dma((spans,)), dma((spans,)), dma,
            dma((spans, heads)), dma((spans, heads)),
            dma((sides, tiles)), dma((sides, tiles)),
            dma((sides,)), dma((spans,)),
            dma((spans, chips)), dma((sides, chips)),
            dma((chips, CUTS)), dma((chips, CUTS)), dma((chips, CUTS)), dma((chips, CUTS)), dma,
        ],
        compiler_params=pltpu.CompilerParams(collective_id=0, has_side_effects=True, vmem_limit_bytes=VMEM_LIMIT),
        name="layer",
    )(layer_input, w_query, w_key, w_value, w_out, log_decay, level_gain, level_mask)
    total = shares[0].astype(full)
    for j in range(chips - 1, 0, -1):
        total = total + shares[j].astype(full)
    return total.astype(half)


def solution(mesh):
    in_specs = (
        P(("ctx", "head"), None),
        P("ctx", "head"),
        P("ctx", "head"),
        P("ctx", "head"),
        P("head", None),
        P("head", "ctx"),
        P("head", None),
        P("ctx", None),
    )
    out_specs = P(("ctx", "head"), None)
    return jax.shard_map(
        on_device, mesh=mesh, in_specs=in_specs, out_specs=out_specs, check_vma=False
    )
```
